512 devices in a mesh: gx: 32 (over z, x), gy: 16 (over y, core).
Axes of the slice: x: 4, y: 8, z: 8, core: 2. Of those that a mesh axis runs over, the one named last changes fastest.
Arguments:
- vel0: bfloat16 [2, 8192, 4096], P(None, 'gx', 'gy'), may hold values from -6 to 6
- visc: float32 [8192, 4096], P('gx', 'gy'), may hold values from 0.1 to 1
- fric: float32 [8192, 4096], P('gx', 'gy'), may hold values from 0.5 to 5
- drive: bfloat16 [2, 8192, 4096], P(None, 'gx', 'gy'), may hold values from -6 to 6
- scene_obs: bfloat16 [16, 512, 2, 128, 128], P('gy', 'gx'), may hold values from -6 to 6
- scene_weight: bfloat16 [16, 512], P('gy', 'gx'), may hold values from 0.5 to 4
- scene_owner: int32 [16, 512, 1], P('gy', 'gx'), may hold values from 0 to 31; in each aligned block of 16 rows (0 to 15, 16 to 31, ..., all dimensions but the last counted through in order) at most 2 rows name the same one
- scene_slot: int32 [16, 512], P('gy', 'gx'), may hold values from 0 to 3
- ice_mask: int32 [64, 32], P('gx', 'gy'), may hold values 0 or 1
Outputs:
- grad_fric: float32 [8192, 4096], P('gx', 'gy')
The draws below stay inside these ranges and needn't reach their ends.
Inputs may be any that keep to these rules, and one draw needn't show every extreme that they name: `scene_owner`: among one device's 16 scenes at most 2 name the same owner, and in some device one owner is named exactly 2 times.
All inputs are finite; a program needn't handle non-finite values. No bound on the sum of `ice_mask` on one device may be relied on, other than what follows from the above.
Results may differ from the reference program's by a relative error of at most 0.0003.
Values may be sent and summed in bfloat16 or wider, within the bound.
A program may use at most 64 MiB of HBM per device.

```python
import math
import jax
import jax.numpy as jnp
import numpy as np
from jax import lax

TILE = 128
NS = 16
CAP = 2
SX = 2
SY = 2
SLOTS = 4
NX = 8192
NY = 4096
SCENES_X = 512
N_GX = 32
N_GY = 16


def plant(array, own_key, low, top_value):
    longest = array.shape.index(max(array.shape))
    spots = []
    for shift in (0, 1):
        where = [jax.random.randint(jax.random.fold_in(own_key, axis), (), 0, length) for axis, length in enumerate(array.shape)]
        where[longest] = (where[longest] + shift) % array.shape[longest]
        spots.append(tuple(where))
    return array.at[spots[0]].set(low).at[spots[1]].set(top_value)


def steps_of(key, shape, split, least, high):
    factor_of, own = 1.0, jax.random.fold_in(key, 6)
    for dim, parts in split:
        draws = jnp.exp(jax.random.uniform(jax.random.fold_in(own, dim), (parts,), jnp.float32, least / len(split), high / len(split)))
        factor_of = factor_of * jnp.repeat(draws, shape[dim] // parts).reshape([-1 if axis == dim else 1 for axis in range(len(shape))])
    return factor_of


def assign_block(stream_key, own, number, rows, amount, top, reach, lean):
    ranking = jax.random.permutation(stream_key, amount)
    crowded, common = load_shares(amount, rows * top, reach, lean, True), load_shares(amount, rows * top, reach, lean, False)
    places = jnp.arange(amount)

    def named(sizes, turn):
        used = int((sizes > 0).sum())
        fixed = max(1, used // 4)
        moved = fixed + (places - fixed + turn * (used - fixed)) % max(1, amount - fixed)
        return jnp.zeros((amount,), jnp.int32).at[ranking[jnp.where(places < fixed, places, moved)]].set(jnp.asarray(sizes, jnp.int32))

    sizes = jnp.where(number % 4 == 0, named(crowded, number // 4), named(common, number - number // 4 - 1))
    mixed = jax.random.permutation(jax.random.fold_in(own, 3), amount)
    giver, sink = mixed[0:amount // 2 * 2:2], mixed[1:amount // 2 * 2:2]
    room = jnp.minimum(sizes[giver] - 1, reach - sizes[sink]) // 2
    room = jnp.where((giver == ranking[0]) | (sink == ranking[0]) | (sizes[sink] == 0), 0, jnp.maximum(room, 0))
    moved = jax.random.randint(jax.random.fold_in(own, 4), (amount // 2,), 0, 1 << 20) % (room + 1)
    sizes = sizes.at[giver].add(-moved).at[sink].add(moved)
    members = jnp.searchsorted(jnp.cumsum(sizes), jnp.arange(rows * top), side="right").astype(jnp.int32)
    listing = members.reshape(top, rows).T
    listing = listing[jax.random.permutation(jax.random.fold_in(own, 1), rows)]
    turn = jax.random.randint(jax.random.fold_in(own, 2), (rows, 1), 0, top)
    return jnp.take_along_axis(listing, (jnp.arange(top)[None, :] + turn) % top, axis=1)


def load_shares(count, total, bound, lean, full):
    loads = [(1 << 20) // math.isqrt(rank ** lean) + 1 for rank in range(1, count + 1)]
    largest = bound if full else min(bound, max(-(-total // count), total * loads[0] // sum(loads)))
    least = 1 if total - largest >= count - 1 else 0
    given, spare = [largest] + [least] * (count - 1), total - largest - least * (count - 1)
    while spare > 0:
        candidates = [i for i in range(1, count) if given[i] < largest] or [i for i in range(1, count) if given[i] < bound]
        whole, budget = sum([loads[i] for i in candidates]), spare
        for i in candidates:
            extra = min(bound - given[i], max(1, budget * loads[i] // whole), spare)
            given[i] = given[i] + extra
            spare = spare - extra
    return np.array(given)


def scatter_about(stream_key, extent, width, most, pieces=(), kind=jnp.bfloat16):
    values = jax.random.normal(stream_key, extent, jnp.float32) * width
    if len(pieces) > 0:
        values = steps_of(stream_key, extent, pieces, -0.22, 0.18) * values
    return jnp.clip(values, min=-most, max=most).astype(kind)


def setup_inputs(seed: int = 0) -> dict:
    seeds = jax.random.split(jax.random.key(seed), 10)
    vel0 = scatter_about(seeds[0], (2, NX, NY), 1.0, 6.0, ((1, 32), (2, 16)))
    visc = jnp.clip(jnp.exp(math.log(1.0) - 2.3025851 * jax.random.uniform(seeds[1], (NX, NY), jnp.float32) ** steps_of(seeds[1], (NX, NY), ((0, 32), (1, 16)), -0.2, 0.2)), 0.1, 1.0)
    fric = jnp.clip(jnp.exp(math.log(5.0) - 2.3025851 * jax.random.uniform(seeds[2], (NX, NY), jnp.float32) ** steps_of(seeds[2], (NX, NY), ((0, 32), (1, 16)), -0.2, 0.2)), 0.5, 5.0)
    drive = scatter_about(seeds[3], (2, NX, NY), 1.0, 6.0, ((1, 32), (2, 16)))
    scene_obs = scatter_about(seeds[4], (N_GY, SCENES_X, 2, TILE, TILE), 1.0, 6.0, ((0, 16), (1, 32)))
    scene_weight = jnp.clip(jnp.exp(math.log(4.0) - 2.0794415 * jax.random.uniform(seeds[5], (N_GY, SCENES_X), jnp.float32) ** steps_of(seeds[5], (N_GY, SCENES_X), ((0, 16), (1, 32)), -0.2, 0.2)), 0.5, 4.0).astype(jnp.bfloat16)
    scene_owner_keys = jax.random.split(jax.random.fold_in(seeds[6], 1), N_GY * SCENES_X // NS)
    scene_owner_turns = jax.random.permutation(jax.random.fold_in(seeds[6], 3), N_GY * SCENES_X // NS)
    scene_owner = jax.vmap(lambda own, number: assign_block(jax.random.fold_in(seeds[6], 2), own, number, NS, N_GX, 1, CAP, 2))(scene_owner_keys, scene_owner_turns).reshape((N_GY, SCENES_X, 1))
    scene_slot = plant(jax.random.randint(seeds[7], (N_GY, SCENES_X), 0, SLOTS), jax.random.fold_in(seeds[7], 1), 0, SLOTS - 1).astype(jnp.int32)
    ice_mask = plant((jax.random.randint(seeds[8], (NX // TILE, NY // TILE), 0, 4) < 3).astype(jnp.int32), jax.random.fold_in(seeds[8], 1), 0, 1)
    return {"vel0": vel0, "visc": visc, "fric": fric, "drive": drive, "scene_obs": scene_obs, "scene_weight": scene_weight, "scene_owner": scene_owner, "scene_slot": scene_slot, "ice_mask": ice_mask}


def upper(a, axis):
    if axis == 0:
        return jnp.concatenate([a[1:], jnp.zeros_like(a[:1])], axis=0)
    return jnp.concatenate([a[:, 1:], jnp.zeros_like(a[:, :1])], axis=1)


def lower(a, axis):
    if axis == 0:
        return jnp.concatenate([jnp.zeros_like(a[:1]), a[:-1]], axis=0)
    return jnp.concatenate([jnp.zeros_like(a[:, :1]), a[:, :-1]], axis=1)


def stress_image(field, visc):
    vel_u = field[0]
    vel_v = field[1]
    a_x = upper(vel_u, 0) - vel_u
    a_y = upper(vel_u, 1) - vel_u
    b_x = upper(vel_v, 0) - vel_v
    b_y = upper(vel_v, 1) - vel_v
    sxx = visc * (4.0 * a_x + 2.0 * b_y)
    syy = visc * (4.0 * b_y + 2.0 * a_x)
    sxy = visc * (a_y + b_x)
    push_u = lower(sxx, 0) - sxx + lower(sxy, 1) - sxy
    push_v = lower(sxy, 0) - sxy + lower(syy, 1) - syy
    return jnp.stack([push_u, push_v])


def reference(vel0, visc, fric, drive, scene_obs, scene_weight, scene_owner, scene_slot, ice_mask):
    visc_x = lower(visc, 0)
    visc_y = lower(visc, 1)
    diag = jnp.stack([5.0 * visc + 4.0 * visc_x + visc_y, 5.0 * visc + visc_x + 4.0 * visc_y])
    relax = 1.0 / (diag + fric)
    start = vel0.astype(jnp.float32)
    force = drive.astype(jnp.float32)
    first_res = force - stress_image(start, visc) - fric * start
    first = start + 0.6 * relax * first_res
    second_res = force - stress_image(first, visc) - fric * first
    second = first + 0.6 * relax * second_res

    owner = scene_owner[:, :, 0].astype(jnp.int32)
    slot = scene_slot.astype(jnp.int32)
    rows = jnp.arange(N_GY, dtype=jnp.int32)[:, None]
    tile_row = (owner * SX + slot // SY).astype(jnp.int32)
    tile_col = (rows * SY + slot % SY).astype(jnp.int32)
    weight = scene_weight.astype(jnp.float32)
    tile_weight = jnp.zeros((NX // TILE, NY // TILE), jnp.float32).at[tile_row, tile_col].add(weight)

    def add_row(index, total):
        index = jnp.asarray(index).astype(jnp.int32)
        obs_row = lax.dynamic_index_in_dim(scene_obs, index, 0, keepdims=False).astype(jnp.float32)
        row_t = lax.dynamic_index_in_dim(tile_row, index, 0, keepdims=False)
        col_t = lax.dynamic_index_in_dim(tile_col, index, 0, keepdims=False)
        weight_row = lax.dynamic_index_in_dim(weight, index, 0, keepdims=False)
        return total.at[row_t, col_t].add(weight_row[:, None, None, None] * obs_row)

    obs_tiles = lax.fori_loop(0, N_GY, add_row, jnp.zeros((NX // TILE, NY // TILE, 2, TILE, TILE), jnp.float32))
    obs_sum = obs_tiles.transpose(2, 0, 3, 1, 4).reshape(2, NX, NY)
    weight_cell = jnp.repeat(jnp.repeat(tile_weight, TILE, axis=0), TILE, axis=1)
    ice = jnp.repeat(jnp.repeat(ice_mask.astype(jnp.float32), TILE, axis=0), TILE, axis=1)

    misfit_grad = ice * (weight_cell * second - obs_sum)
    lift_two = 0.6 * relax * misfit_grad
    back = misfit_grad - stress_image(lift_two, visc) - fric * lift_two
    lift_one = 0.6 * relax * back
    part_one = jnp.sum(lift_one * (relax * first_res + start), axis=0)
    part_two = jnp.sum(lift_two * (relax * second_res + first), axis=0)
    return -ice * (part_one + part_two)
```

```python
import functools

import jax
import jax.numpy as jnp
from jax import lax
from jax.experimental import pallas as pl
from jax.experimental.pallas import tpu as pltpu
from jax.sharding import PartitionSpec as P

OMEGA = 0.6
NX, NZ = 4, 8
SLOTS = 4
ROWS = 16
LEAD = 2
GAP = 1
MESH = pl.DeviceIdType.MESH


def from_behind(value, axis, steps):
    count = lax.axis_size(axis)
    first, last = (max(0, -steps), min(count, count - steps))
    return lax.ppermute(value, axis, [(source, source + steps) for source in range(first, last)])


def exchange_kernel(
    meta_ref, obs_ref, out_ref, wsum_ref,
    meta, ag, table, part, part_w, rp1, rp, rm1, rm, rw,
    own_sem, meta_s, meta_r, ag_s, ag_r, rs_s, rs_r, rw_s, rw_r,
):
    chunks = ag.shape[1]
    scenes = ag.shape[2]
    half = scenes // 2
    me_x, me_y = lax.axis_index("gx"), lax.axis_index("gy")
    x, z = lax.rem(me_x, NX), me_x // NX
    x_right = (z * NX + lax.rem(x + 1, NX), me_y)
    x_left = (z * NX + lax.rem(x + NX - 1, NX), me_y)
    x_far = (z * NX + lax.rem(x + 2, NX), me_y)
    z_right = (lax.rem(z + 1, NZ) * NX + x, me_y)
    z_left = (lax.rem(z + NZ - 1, NZ) * NX + x, me_y)

    def remote(src, dst, send, recv, device):
        return pltpu.make_async_remote_copy(
            src_ref=src, dst_ref=dst, send_sem=send, recv_sem=recv, device_id=device, device_id_type=MESH
        )

    def rows(c):
        return pl.ds(pl.multiple_of(c * ROWS, ROWS), ROWS)

    def own_load(c):
        return pltpu.make_async_copy(obs_ref.at[:, rows(c), :], ag.at[0, c], own_sem.at[c])

    def own_send(side, c):
        return remote(
            obs_ref.at[:, rows(c), :], ag.at[1 + side, c], ag_s.at[side, c], ag_r.at[side, c],
            (x_right, x_left)[side],
        )

    def far_send(side, c):
        piece = pl.ds(side * half, half)
        return remote(
            ag.at[1 + side, c, piece], ag.at[3, c, piece], ag_s.at[2 + side, c], ag_r.at[2 + side, c],
            (x_right, x_left)[side],
        )

    def meta_send(peer):
        return remote(
            meta_ref, meta.at[peer], meta_s.at[peer], meta_r.at[peer], (x_right, x_left, x_far)[peer]
        )

    def ring_send(side, stage, c):
        device = (z_right, z_left)[side]
        semaphores = (rs_s.at[side * 4 + stage - 1, c], rs_r.at[side * 4 + stage - 1, c])
        if stage == 1:
            return remote(
                part.at[c, 4, pl.ds(side * 2, 2)], (rp1, rm1)[side].at[c], *semaphores, device
            )
        source = 5 - stage if side == 0 else 3 + stage
        return remote(part.at[c, source], (rp, rm)[side].at[stage - 2, c], *semaphores, device)

    def ring_send_w(side, stage):
        source = 5 - stage if side == 0 else (8 if stage == 1 else 3 + stage)
        index = side * 4 + stage - 1
        return remote(
            part_w.at[source], rw.at[index], rw_s.at[index], rw_r.at[index], (z_right, z_left)[side]
        )

    barrier = pltpu.get_barrier_semaphore()
    for device in (x_right, x_left, x_far, z_right, z_left):
        pl.semaphore_signal(barrier, inc=1, device_id=device, device_id_type=MESH)
    for c in range(chunks):
        own_load(c).start()
    pl.semaphore_wait(barrier, 5)

    for peer in range(3):
        meta_send(peer).start()
    for c in range(LEAD):
        own_send(0, c).start()
        own_send(1, c).start()

    width = scenes * ROWS
    count = NZ * SLOTS * ROWS

    def fill(source, block):
        key, weight = block[0:1, :], block[1:2, :]
        row = lax.broadcasted_iota(jnp.int32, (count, 1), 0)
        lane = lax.broadcasted_iota(jnp.int32, (1, width), 1)
        target_z = lax.rem(z + row // (SLOTS * ROWS), NZ)
        want = (target_z * NX + x) * SLOTS + lax.rem(row // ROWS, SLOTS)
        want = want.astype(jnp.float32)
        hit = jnp.logical_and(key == want, lax.rem(lane, ROWS) == lax.rem(row, ROWS))
        table[:, source * width : (source + 1) * width] = jnp.where(hit, weight, 0.0).astype(jnp.bfloat16)
        row = lax.broadcasted_iota(jnp.int32, (NZ * 8, 1), 0)
        slot = lax.rem(row, 8)
        target_z = lax.rem(z + row // 8, NZ)
        want = jnp.where(slot < SLOTS, (target_z * NX + x) * SLOTS + slot, -1).astype(jnp.float32)
        hit = jnp.logical_and(key == want, lax.rem(lane, ROWS) == 0)
        return jnp.sum(jnp.where(hit, weight, 0.0), axis=1, keepdims=True)

    total_w = fill(0, meta_ref[...])
    for peer in range(3):
        meta_send(peer).wait_recv()
        total_w = total_w + fill(1 + peer, meta[peer])
    total_w = jnp.broadcast_to(total_w, (NZ * 8, 128)).reshape(NZ, 8, 128)
    part_w[0:NZ] = total_w
    slot = lax.broadcasted_iota(jnp.int32, (8, 128), 0)
    part_w[4] = jnp.where(slot < 2, total_w[4], 0.0)
    part_w[8] = jnp.where(slot < 2, 0.0, total_w[4])
    ring_send_w(0, 1).start()
    ring_send_w(1, 1).start()
    for c in range(chunks):
        own_load(c).wait()

    def at_chunk(c, action):
        pl.when(jnp.logical_and(c >= 0, c < chunks))(lambda: action(c))

    def combine(c):
        for side in range(2):
            far_send(side, c).wait_recv()
        columns = []
        for h in range(ROWS // 16):
            columns.append(
                jnp.concatenate(
                    [ag[s, c, :, h * 16 : (h + 1) * 16, :].reshape(scenes * 16, 128) for s in range(4)], axis=0
                )
            )
        stacked = columns[0] if len(columns) == 1 else jnp.concatenate(columns, axis=1)
        sums = jnp.dot(table[...], stacked, preferred_element_type=jnp.float32)
        part[c] = sums.reshape(NZ, SLOTS, ROWS, 128)
        ring_send(0, 1, c).start()
        ring_send(1, 1, c).start()

    def ring_step(stage, c):
        for side in range(2):
            ring_send(side, stage - 1, c).wait_recv()
            mine = 5 - stage if side == 0 else 3 + stage
            if stage == 2:
                part[c, mine, side * 2 : side * 2 + 2] += (rp1, rm1)[side][c]
            else:
                part[c, mine] += (rp, rm)[side][stage - 3, c]
            ring_send(side, stage, c).start()

    def finish(c):
        for side in range(2):
            ring_send(side, 4, c).wait_recv()
        out_ref[:, rows(c), :] = part[c, 0] + (rp[2, c] + rm[2, c])

    def ring_step_w(stage):
        for side in range(2):
            ring_send_w(side, stage - 1).wait_recv()
            mine = 5 - stage if side == 0 else 3 + stage
            part_w[mine] += rw[side * 4 + stage - 2]
            ring_send_w(side, stage).start()

    def step(k, carry):
        @pl.when(k + LEAD < chunks)
        def _():
            own_send(0, k + LEAD).start()
            own_send(1, k + LEAD).start()

        @pl.when(k < chunks)
        def _():
            for side in range(2):
                own_send(side, k).wait_recv()
                far_send(side, k).start()

        at_chunk(k - 1 - 4 * GAP, finish)
        for stage in (4, 3, 2):
            at_chunk(k - 1 - (stage - 1) * GAP, functools.partial(ring_step, stage))
            pl.when(k == stage + 1)(functools.partial(ring_step_w, stage))
        at_chunk(k - 1, combine)
        return carry

    lax.fori_loop(0, chunks + 1 + 4 * GAP, step, 0)
    for side in range(2):
        ring_send_w(side, 4).wait_recv()
    wsum_ref[...] = part_w[0] + (rw[3] + rw[7])

    def drain(c, carry):
        for side in range(2):
            own_send(side, c).wait_send()
            far_send(side, c).wait_send()
            for stage in range(1, 5):
                ring_send(side, stage, c).wait_send()
        return carry

    lax.fori_loop(0, chunks, drain, 0)
    for peer in range(3):
        meta_send(peer).wait_send()
    for side in range(2):
        for stage in range(1, 5):
            ring_send_w(side, stage).wait_send()


def exchange(obs, owners, slots, weights):
    scenes, _, tile, _ = obs.shape
    height = 2 * tile
    chunks = height // ROWS
    key = jnp.repeat((owners * SLOTS + slots).astype(jnp.float32), ROWS)
    weight = jnp.repeat(weights.astype(jnp.float32), ROWS)
    meta = jnp.concatenate([key[None], weight[None], jnp.zeros((6, scenes * ROWS), jnp.float32)], axis=0)
    f32, bf16 = jnp.float32, jnp.bfloat16
    dma = pltpu.SemaphoreType.DMA
    return pl.pallas_call(
        exchange_kernel,
        out_shape=(
            jax.ShapeDtypeStruct((SLOTS, height, tile), f32),
            jax.ShapeDtypeStruct((8, 128), f32),
        ),
        in_specs=[pl.BlockSpec(memory_space=pltpu.VMEM), pl.BlockSpec(memory_space=pl.ANY)],
        out_specs=(pl.BlockSpec(memory_space=pltpu.VMEM), pl.BlockSpec(memory_space=pltpu.VMEM)),
        scratch_shapes=[
            pltpu.VMEM((3, 8, scenes * ROWS), f32),
            pltpu.VMEM((4, chunks, scenes, ROWS, tile), bf16),
            pltpu.VMEM((NZ * SLOTS * ROWS, 4 * scenes * ROWS), bf16),
            pltpu.VMEM((chunks, NZ, SLOTS, ROWS, tile), f32),
            pltpu.VMEM((NZ + 1, 8, 128), f32),
            pltpu.VMEM((chunks, 2, ROWS, tile), f32),
            pltpu.VMEM((3, chunks, SLOTS, ROWS, tile), f32),
            pltpu.VMEM((chunks, 2, ROWS, tile), f32),
            pltpu.VMEM((3, chunks, SLOTS, ROWS, tile), f32),
            pltpu.VMEM((8, 8, 128), f32),
            dma((chunks,)),
            dma((3,)), dma((3,)),
            dma((4, chunks)), dma((4, chunks)),
            dma((8, chunks)), dma((8, chunks)),
            dma((8,)), dma((8,)),
        ],
        compiler_params=pltpu.CompilerParams(
            collective_id=0, has_side_effects=True, vmem_limit_bytes=48 * 1024 * 1024
        ),
    )(meta, obs.reshape(scenes, height, tile))


def stress_image(field, visc):
    above_x = from_behind(field[:, :1, :], "gx", -1)
    above_y = from_behind(field[:, :, :1], "gy", -1)
    along_x = jnp.concatenate([field[:, 1:, :], above_x], axis=1) - field
    along_y = jnp.concatenate([field[:, :, 1:], above_y], axis=2) - field
    sxx = visc * (4.0 * along_x[0] + 2.0 * along_y[1])
    syy = visc * (4.0 * along_y[1] + 2.0 * along_x[0])
    sxy = visc * (along_y[0] + along_x[1])
    below_x = from_behind(jnp.stack([sxx[-1], sxy[-1]]), "gx", 1)
    below_y = from_behind(jnp.stack([sxy[:, -1], syy[:, -1]]), "gy", 1)
    push_u = (
        jnp.concatenate([below_x[0:1], sxx[:-1]], axis=0)
        - sxx
        + jnp.concatenate([below_y[0][:, None], sxy[:, :-1]], axis=1)
        - sxy
    )
    push_v = (
        jnp.concatenate([below_x[1:2], sxy[:-1]], axis=0)
        - sxy
        + jnp.concatenate([below_y[1][:, None], syy[:, :-1]], axis=1)
        - syy
    )
    return jnp.stack([push_u, push_v])


def spread_tiles(values, tiles_x, tiles_y, tile):
    wide = jnp.broadcast_to(values.reshape(tiles_x, 1, tiles_y, 1), (tiles_x, tile, tiles_y, tile))
    return wide.reshape(tiles_x * tile, tiles_y * tile)


def body(vel0, visc, fric, drive, scene_obs, scene_weight, scene_owner, scene_slot, ice_mask):
    cells_x, cells_y = visc.shape
    tile = scene_obs.shape[-1]
    tiles_x = cells_x // tile
    tiles_y = cells_y // tile
    summed, tile_weight = exchange(scene_obs[0], scene_owner[0, :, 0], scene_slot[0], scene_weight[0])
    visc_row = from_behind(visc[-1:, :], "gx", 1)
    visc_col = from_behind(visc[:, -1:], "gy", 1)
    visc_x = jnp.concatenate([visc_row, visc[:-1]], axis=0)
    visc_y = jnp.concatenate([visc_col, visc[:, :-1]], axis=1)
    diag = jnp.stack([5.0 * visc + 4.0 * visc_x + visc_y, 5.0 * visc + visc_x + 4.0 * visc_y])
    relax = 1.0 / (diag + fric)
    start = vel0.astype(jnp.float32)
    force = drive.astype(jnp.float32)
    first_res = force - stress_image(start, visc) - fric * start
    first = start + OMEGA * relax * first_res
    second_res = force - stress_image(first, visc) - fric * first
    second = first + OMEGA * relax * second_res
    obs_sum = (
        summed.reshape(tiles_x, tiles_y, 2, tile, tile)
        .transpose(2, 0, 3, 1, 4)
        .reshape(2, cells_x, cells_y)
    )
    weight_cell = spread_tiles(tile_weight[:SLOTS, 0], tiles_x, tiles_y, tile)
    ice = spread_tiles(ice_mask.astype(jnp.float32), tiles_x, tiles_y, tile)
    misfit_grad = ice * (weight_cell * second - obs_sum)
    lift_two = OMEGA * relax * misfit_grad
    back = misfit_grad - stress_image(lift_two, visc) - fric * lift_two
    lift_one = OMEGA * relax * back
    part_one = jnp.sum(lift_one * (relax * first_res + start), axis=0)
    part_two = jnp.sum(lift_two * (relax * second_res + first), axis=0)
    return -ice * (part_one + part_two)


def solution(mesh):
    placed = (
        P(None, "gx", "gy"),
        P("gx", "gy"),
        P("gx", "gy"),
        P(None, "gx", "gy"),
        P("gy", "gx", None, None, None),
        P("gy", "gx"),
        P("gy", "gx", None),
        P("gy", "gx"),
        P("gx", "gy"),
    )
    return jax.shard_map(body, mesh=mesh, in_specs=placed, out_specs=P("gx", "gy"), check_vma=False)
```

```python
import functools

import jax
import jax.numpy as jnp
from jax import lax
from jax.experimental import pallas as pl
from jax.experimental.pallas import tpu as pltpu
from jax.sharding import PartitionSpec as P

OMEGA = 0.6
NX, NZ = 4, 8
SLOTS = 4
ROWS = 16
LEAD = 2
GAP = 1
MESH = pl.DeviceIdType.MESH


def exchange_kernel(
    meta_ref, ice_ref, vel_ref, visc_ref, fric_ref, drive_ref, obs_ref, out_ref,
    relax, first, second, q_one, q_two, misfit, lift, edge, halo,
    meta, ag, table, part, part_w, rp1, rp, rm1, rm, rw,
    own_sem, meta_s, meta_r, ag_s, ag_r, rs_s, rs_r, rw_s, rw_r, edge_s, edge_r,
):
    chunks = ag.shape[1]
    scenes = ag.shape[2]
    half = scenes // 2
    me_x, me_y = lax.axis_index("gx"), lax.axis_index("gy")
    x, z = lax.rem(me_x, NX), me_x // NX
    x_right = (z * NX + lax.rem(x + 1, NX), me_y)
    x_left = (z * NX + lax.rem(x + NX - 1, NX), me_y)
    x_far = (z * NX + lax.rem(x + 2, NX), me_y)
    z_right = (lax.rem(z + 1, NZ) * NX + x, me_y)
    z_left = (lax.rem(z + NZ - 1, NZ) * NX + x, me_y)

    gx_next, gx_back = lax.rem(me_x + 1, NX * NZ), lax.rem(me_x + NX * NZ - 1, NX * NZ)
    side_y = lax.axis_size("gy")
    gy_next, gy_back = lax.rem(me_y + 1, side_y), lax.rem(me_y + side_y - 1, side_y)
    at_first_x, at_last_x = me_x == 0, me_x == NX * NZ - 1
    at_first_y, at_last_y = me_y == 0, me_y == side_y - 1
    edges = (
        (0, (gx_back, me_y)),
        (1, (gx_next, me_y)),
        (2, (me_x, gy_back)),
        (3, (me_x, gy_next)),
        (1, (gx_next, gy_back)),
        (0, (gx_back, gy_next)),
    )

    def remote(src, dst, send, recv, device):
        return pltpu.make_async_remote_copy(
            src_ref=src, dst_ref=dst, send_sem=send, recv_sem=recv, device_id=device, device_id_type=MESH
        )

    def rows(c):
        return pl.ds(pl.multiple_of(c * ROWS, ROWS), ROWS)

    def own_load(c):
        return pltpu.make_async_copy(obs_ref.at[:, rows(c), :], ag.at[0, c], own_sem.at[c])

    def own_send(side, c):
        return remote(
            obs_ref.at[:, rows(c), :], ag.at[1 + side, c], ag_s.at[side, c], ag_r.at[side, c],
            (x_right, x_left)[side],
        )

    def far_send(side, c):
        piece = pl.ds(side * half, half)
        return remote(
            ag.at[1 + side, c, piece], ag.at[3, c, piece], ag_s.at[2 + side, c], ag_r.at[2 + side, c],
            (x_right, x_left)[side],
        )

    def meta_send(peer):
        return remote(
            meta_ref, meta.at[peer], meta_s.at[peer], meta_r.at[peer], (x_right, x_left, x_far)[peer]
        )

    def ring_send(side, stage, c):
        device = (z_right, z_left)[side]
        semaphores = (rs_s.at[side * 4 + stage - 1, c], rs_r.at[side * 4 + stage - 1, c])
        if stage == 1:
            return remote(
                part.at[c, 4, pl.ds(side * 2, 2)], (rp1, rm1)[side].at[c], *semaphores, device
            )
        source = 5 - stage if side == 0 else 3 + stage
        return remote(part.at[c, source], (rp, rm)[side].at[stage - 2, c], *semaphores, device)

    def ring_send_w(side, stage):
        source = 5 - stage if side == 0 else (8 if stage == 1 else 3 + stage)
        index = side * 4 + stage - 1
        return remote(
            part_w.at[source], rw.at[index], rw_s.at[index], rw_r.at[index], (z_right, z_left)[side]
        )

    def edge_send(e, place):
        message, device = edges[place]
        return remote(
            edge.at[e, message], halo.at[e, place], edge_s.at[e, place], edge_r.at[e, place], device
        )

    barrier = pltpu.get_barrier_semaphore()
    for device in (x_right, x_left, x_far, z_right, z_left, *(device for _, device in edges)):
        pl.semaphore_signal(barrier, inc=1, device_id=device, device_id_type=MESH)
    for c in range(chunks):
        own_load(c).start()
    pl.semaphore_wait(barrier, 11)

    for peer in range(3):
        meta_send(peer).start()
    for c in range(LEAD):
        own_send(0, c).start()
        own_send(1, c).start()

    cells = visc_ref.shape[0]
    row_of = lax.broadcasted_iota(jnp.int32, (cells, 1), 0)
    lane_of = lax.broadcasted_iota(jnp.int32, (1, cells), 1)

    def send_edges(e, u, v, visc=None):
        edge[e, 0, 0:1, :] = u[0:1, :]
        edge[e, 0, 1:2, :] = v[0:1, :]
        edge[e, 1, 0:1, :] = u[cells - 1 :, :]
        edge[e, 1, 1:2, :] = v[cells - 1 :, :]
        lane = lane_of[:, :128]
        packed = jnp.where(lane == 0, u[:, :128], pltpu.roll(v[:, :128], 1, 1))
        packed = jnp.where(lane == 2, pltpu.roll(u[:, cells - 128 :], 3, 1), packed)
        packed = jnp.where(lane == 3, pltpu.roll(v[:, cells - 128 :], 4, 1), packed)
        if visc is not None:
            edge[e, 1, 2:3, :] = visc[cells - 1 :, :]
            packed = jnp.where(lane == 4, pltpu.roll(visc[:, cells - 128 :], 5, 1), packed)
        turned = packed.T
        edge[e, 2, 0:2, :] = turned[0:2]
        edge[e, 3, 0:3, :] = turned[2:5]
        for place in range(6):
            edge_send(e, place).start()

    def lower_x(field, row):
        return jnp.where(row_of == 0, row, pltpu.roll(field, 1, 0))

    def lower_y(field, column):
        return jnp.where(lane_of == 0, column, pltpu.roll(field, 1, 1))

    def stress_image(e, u, v, visc):
        for place in range(6):
            edge_send(e, place).wait_recv()

        def got(place, r):
            return halo[e, place, r : r + 1, :]

        zero = jnp.zeros((1, cells), jnp.float32)
        up_x = [jnp.where(at_last_x, zero, got(0, r)) for r in range(2)]
        up_y = [jnp.where(at_last_y, zero, got(2, r)) for r in range(2)]
        visc_x = jnp.where(at_first_x, zero, halo[0, 1, 2:3, :])
        visc_y = jnp.where(at_first_y, zero, halo[0, 3, 2:3, :])
        back_x = [got(1, r) for r in range(2)]
        back_y = [got(3, r) for r in range(2)]
        back_x_up, back_y_up = [], []
        for r in range(2):
            corner = jnp.where(at_last_y, 0.0, halo[e, 4, r : r + 1, 0:1])
            back_x_up.append(jnp.where(lane_of == cells - 1, corner, pltpu.roll(back_x[r], cells - 1, 1)))
            corner = jnp.where(at_last_x, 0.0, halo[e, 5, r : r + 1, cells - 1 : cells])
            back_y_up.append(jnp.where(lane_of == cells - 1, corner, pltpu.roll(back_y[r], cells - 1, 1)))
        sxx_x = visc_x * (4.0 * (u[0:1, :] - back_x[0]) + 2.0 * (back_x_up[1] - back_x[1]))
        sxy_x = visc_x * ((back_x_up[0] - back_x[0]) + (v[0:1, :] - back_x[1]))
        u_y, v_y = edge[e, 2, 0:1, :], edge[e, 2, 1:2, :]
        sxy_y = visc_y * ((u_y - back_y[0]) + (back_y_up[1] - back_y[1]))
        syy_y = visc_y * (4.0 * (v_y - back_y[1]) + 2.0 * (back_y_up[0] - back_y[0]))
        columns = jnp.concatenate([up_y[0], up_y[1], sxy_y, syy_y, visc_y, zero, zero, zero], axis=0).T
        column = [columns[:, r : r + 1] for r in range(5)]
        a_x = jnp.where(row_of == cells - 1, up_x[0], pltpu.roll(u, cells - 1, 0)) - u
        b_x = jnp.where(row_of == cells - 1, up_x[1], pltpu.roll(v, cells - 1, 0)) - v
        a_y = jnp.where(lane_of == cells - 1, column[0], pltpu.roll(u, cells - 1, 1)) - u
        b_y = jnp.where(lane_of == cells - 1, column[1], pltpu.roll(v, cells - 1, 1)) - v
        sxx = visc * (4.0 * a_x + 2.0 * b_y)
        syy = visc * (4.0 * b_y + 2.0 * a_x)
        sxy = visc * (a_y + b_x)
        push_u = lower_x(sxx, sxx_x) - sxx + lower_y(sxy, column[2]) - sxy
        push_v = lower_x(sxy, sxy_x) - sxy + lower_y(syy, column[3]) - syy
        return (push_u, push_v), visc_x, column[4]

    def first_sweep():
        visc, fric = visc_ref[...], fric_ref[...]
        start = [vel_ref[r].astype(jnp.float32) for r in range(2)]
        push, row, column = stress_image(0, start[0], start[1], visc)
        visc_x, visc_y = lower_x(visc, row), lower_y(visc, column)
        diag = (5.0 * visc + 4.0 * visc_x + visc_y, 5.0 * visc + visc_x + 4.0 * visc_y)
        for r in range(2):
            relax_r = 1.0 / (diag[r] + fric)
            relax[r] = relax_r
            moved = relax_r * (drive_ref[r].astype(jnp.float32) - push[r] - fric * start[r])
            q_one[r] = moved + start[r]
            first[r] = start[r] + OMEGA * moved
        send_edges(1, first[0], first[1])

    def second_sweep():
        fric = fric_ref[...]
        push, _, _ = stress_image(1, first[0], first[1], visc_ref[...])
        for r in range(2):
            moved = relax[r] * (drive_ref[r].astype(jnp.float32) - push[r] - fric * first[r])
            q_two[r] = moved + first[r]
            second[r] = first[r] + OMEGA * moved

    def adjoint():
        fric = fric_ref[...]
        u, v = lift[0], lift[1]
        send_edges(2, u, v)
        push, _, _ = stress_image(2, u, v, visc_ref[...])
        total = None
        for r in range(2):
            lift_one = OMEGA * relax[r] * (misfit[r] - push[r] - fric * lift[r])
            term = lift_one * q_one[r] + lift[r] * q_two[r]
            total = term if total is None else total + term
        tile = cells // 2
        for s in range(SLOTS):
            i, j = s // 2 * tile, s % 2 * tile
            out_ref[i : i + tile, j : j + tile] = -ice(s) * total[i : i + tile, j : j + tile]

    def ice(s):
        return ice_ref[s // 2, s % 2].astype(jnp.float32)

    width = scenes * ROWS
    count = NZ * SLOTS * ROWS

    def fill(source, block):
        key, weight = block[0:1, :], block[1:2, :]
        row = lax.broadcasted_iota(jnp.int32, (count, 1), 0)
        lane = lax.broadcasted_iota(jnp.int32, (1, width), 1)
        target_z = lax.rem(z + row // (SLOTS * ROWS), NZ)
        want = (target_z * NX + x) * SLOTS + lax.rem(row // ROWS, SLOTS)
        want = want.astype(jnp.float32)
        hit = jnp.logical_and(key == want, lax.rem(lane, ROWS) == lax.rem(row, ROWS))
        table[:, source * width : (source + 1) * width] = jnp.where(hit, weight, 0.0).astype(jnp.bfloat16)
        row = lax.broadcasted_iota(jnp.int32, (NZ * 8, 1), 0)
        slot = lax.rem(row, 8)
        target_z = lax.rem(z + row // 8, NZ)
        want = jnp.where(slot < SLOTS, (target_z * NX + x) * SLOTS + slot, -1).astype(jnp.float32)
        hit = jnp.logical_and(key == want, lax.rem(lane, ROWS) == 0)
        return jnp.sum(jnp.where(hit, weight, 0.0), axis=1, keepdims=True)

    total_w = fill(0, meta_ref[...])
    for peer in range(3):
        meta_send(peer).wait_recv()
        total_w = total_w + fill(1 + peer, meta[peer])
    total_w = jnp.broadcast_to(total_w, (NZ * 8, 128)).reshape(NZ, 8, 128)
    part_w[0:NZ] = total_w
    slot = lax.broadcasted_iota(jnp.int32, (8, 128), 0)
    part_w[4] = jnp.where(slot < 2, total_w[4], 0.0)
    part_w[8] = jnp.where(slot < 2, 0.0, total_w[4])
    ring_send_w(0, 1).start()
    ring_send_w(1, 1).start()
    for c in range(chunks):
        own_load(c).wait()
    send_edges(0, vel_ref[0].astype(jnp.float32), vel_ref[1].astype(jnp.float32), visc_ref[...])

    def at_chunk(c, action):
        pl.when(jnp.logical_and(c >= 0, c < chunks))(lambda: action(c))

    def combine(c):
        for side in range(2):
            far_send(side, c).wait_recv()
        columns = []
        for h in range(ROWS // 16):
            columns.append(
                jnp.concatenate(
                    [ag[s, c, :, h * 16 : (h + 1) * 16, :].reshape(scenes * 16, 128) for s in range(4)], axis=0
                )
            )
        stacked = columns[0] if len(columns) == 1 else jnp.concatenate(columns, axis=1)
        sums = jnp.dot(table[...], stacked, preferred_element_type=jnp.float32)
        part[c] = sums.reshape(NZ, SLOTS, ROWS, 128)
        ring_send(0, 1, c).start()
        ring_send(1, 1, c).start()

    def ring_step(stage, c):
        for side in range(2):
            ring_send(side, stage - 1, c).wait_recv()
            mine = 5 - stage if side == 0 else 3 + stage
            if stage == 2:
                part[c, mine, side * 2 : side * 2 + 2] += (rp1, rm1)[side][c]
            else:
                part[c, mine] += (rp, rm)[side][stage - 3, c]
            ring_send(side, stage, c).start()

    def finish(c):
        for side in range(2):
            ring_send(side, 4, c).wait_recv()
        obs_sum = part[c, 0] + (rp[2, c] + rm[2, c])
        tile = cells // 2
        component = c // (chunks // 2)
        offset = lax.rem(c, chunks // 2) * ROWS
        for s in range(SLOTS):
            at = (
                component,
                pl.ds(pl.multiple_of(s // 2 * tile + offset, ROWS), ROWS),
                slice(s % 2 * tile, s % 2 * tile + tile),
            )
            value = ice(s) * (part_w[0, s : s + 1, :] * second[at] - obs_sum[s])
            misfit[at] = value
            lift[at] = OMEGA * relax[at] * value

    def ring_step_w(stage):
        for side in range(2):
            ring_send_w(side, stage - 1).wait_recv()
            mine = 5 - stage if side == 0 else 3 + stage
            part_w[mine] += rw[side * 4 + stage - 2]
            ring_send_w(side, stage).start()

    def finish_w():
        for side in range(2):
            ring_send_w(side, 4).wait_recv()
        part_w[0] += rw[3] + rw[7]

    def step(k, carry):
        @pl.when(k + LEAD < chunks)
        def _():
            own_send(0, k + LEAD).start()
            own_send(1, k + LEAD).start()

        @pl.when(k < chunks)
        def _():
            for side in range(2):
                own_send(side, k).wait_recv()
                far_send(side, k).start()

        pl.when(k == 1 + 4 * GAP)(finish_w)
        at_chunk(k - 1 - 4 * GAP, finish)
        for stage in (4, 3, 2):
            at_chunk(k - 1 - (stage - 1) * GAP, functools.partial(ring_step, stage))
            pl.when(k == stage - 1)(functools.partial(ring_step_w, stage))
        at_chunk(k - 1, combine)
        pl.when(k == 1)(first_sweep)
        pl.when(k == 3)(second_sweep)
        return carry

    lax.fori_loop(0, chunks + 1 + 4 * GAP, step, 0)
    adjoint()

    def drain(c, carry):
        for side in range(2):
            own_send(side, c).wait_send()
            far_send(side, c).wait_send()
            for stage in range(1, 5):
                ring_send(side, stage, c).wait_send()
        return carry

    lax.fori_loop(0, chunks, drain, 0)
    for peer in range(3):
        meta_send(peer).wait_send()
    for side in range(2):
        for stage in range(1, 5):
            ring_send_w(side, stage).wait_send()
    for e in range(3):
        for place in range(6):
            edge_send(e, place).wait_send()


def body(vel0, visc, fric, drive, scene_obs, scene_weight, scene_owner, scene_slot, ice_mask):
    obs, owners, slots, weights = scene_obs[0], scene_owner[0, :, 0], scene_slot[0], scene_weight[0]
    cells = visc.shape[0]
    scenes, _, tile, _ = obs.shape
    height = 2 * tile
    chunks = height // ROWS
    key = jnp.repeat((owners * SLOTS + slots).astype(jnp.float32), ROWS)
    weight = jnp.repeat(weights.astype(jnp.float32), ROWS)
    meta = jnp.concatenate([key[None], weight[None], jnp.zeros((6, scenes * ROWS), jnp.float32)], axis=0)
    f32, bf16 = jnp.float32, jnp.bfloat16
    dma = pltpu.SemaphoreType.DMA
    return pl.pallas_call(
        exchange_kernel,
        out_shape=jax.ShapeDtypeStruct((cells, cells), f32),
        in_specs=[
            pl.BlockSpec(memory_space=pltpu.VMEM),
            pl.BlockSpec(memory_space=pltpu.SMEM),
            *[pl.BlockSpec(memory_space=pltpu.VMEM)] * 4,
            pl.BlockSpec(memory_space=pl.ANY),
        ],
        out_specs=pl.BlockSpec(memory_space=pltpu.VMEM),
        scratch_shapes=[
            *[pltpu.VMEM((2, cells, cells), f32)] * 7,
            pltpu.VMEM((3, 4, 8, cells), f32),
            pltpu.VMEM((3, 6, 8, cells), f32),
            pltpu.VMEM((3, 8, scenes * ROWS), f32),
            pltpu.VMEM((4, chunks, scenes, ROWS, tile), bf16),
            pltpu.VMEM((NZ * SLOTS * ROWS, 4 * scenes * ROWS), bf16),
            pltpu.VMEM((chunks, NZ, SLOTS, ROWS, tile), f32),
            pltpu.VMEM((NZ + 1, 8, 128), f32),
            pltpu.VMEM((chunks, 2, ROWS, tile), f32),
            pltpu.VMEM((3, chunks, SLOTS, ROWS, tile), f32),
            pltpu.VMEM((chunks, 2, ROWS, tile), f32),
            pltpu.VMEM((3, chunks, SLOTS, ROWS, tile), f32),
            pltpu.VMEM((8, 8, 128), f32),
            dma((chunks,)),
            dma((3,)), dma((3,)),
            dma((4, chunks)), dma((4, chunks)),
            dma((8, chunks)), dma((8, chunks)),
            dma((8,)), dma((8,)),
            dma((3, 6)), dma((3, 6)),
        ],
        compiler_params=pltpu.CompilerParams(
            collective_id=0, has_side_effects=True, vmem_limit_bytes=48 * 1024 * 1024
        ),
    )(meta, ice_mask, vel0, visc, fric, drive, obs.reshape(scenes, height, tile))


def solution(mesh):
    placed = (
        P(None, "gx", "gy"),
        P("gx", "gy"),
        P("gx", "gy"),
        P(None, "gx", "gy"),
        P("gy", "gx", None, None, None),
        P("gy", "gx"),
        P("gy", "gx", None),
        P("gy", "gx"),
        P("gx", "gy"),
    )
    return jax.shard_map(body, mesh=mesh, in_specs=placed, out_specs=P("gx", "gy"), check_vma=False)
```

```python
import functools

import jax
import jax.numpy as jnp
from jax import lax
from jax.experimental import pallas as pl
from jax.experimental.pallas import tpu as pltpu
from jax.sharding import PartitionSpec as P

OMEGA = 0.6
NX, NZ = 4, 8
SLOTS = 4
ROWS = 16
LEAD = 3
GAP = 2
MESH = pl.DeviceIdType.MESH


def exchange_kernel(
    owner_in, slot_in, weight_in, ice_in, vel_in, visc_in, fric_in, drive_in, obs_ref, out_ref,
    owner_ref, slot_ref, weight_ref, ice_ref, vel_ref, visc_ref, fric_ref, drive_ref, meta_ref,
    relax, first, second, q_one, q_two, misfit, lift, edge, halo,
    meta, ag, table, part, part_w, rp1, rp, rm1, rm, rw,
    own_sem, meta_s, meta_r, ag_s, ag_r, rs_s, rs_r, rw_s, rw_r, edge_s, edge_r, load_sem,
):
    chunks = ag.shape[1]
    scenes = ag.shape[2]
    half = scenes // 2
    me_x, me_y = lax.axis_index("gx"), lax.axis_index("gy")
    x, z = lax.rem(me_x, NX), me_x // NX
    x_right = (z * NX + lax.rem(x + 1, NX), me_y)
    x_left = (z * NX + lax.rem(x + NX - 1, NX), me_y)
    x_far = (z * NX + lax.rem(x + 2, NX), me_y)
    z_right = (lax.rem(z + 1, NZ) * NX + x, me_y)
    z_left = (lax.rem(z + NZ - 1, NZ) * NX + x, me_y)

    gx_next, gx_back = lax.rem(me_x + 1, NX * NZ), lax.rem(me_x + NX * NZ - 1, NX * NZ)
    side_y = lax.axis_size("gy")
    gy_next, gy_back = lax.rem(me_y + 1, side_y), lax.rem(me_y + side_y - 1, side_y)
    at_first_x, at_last_x = me_x == 0, me_x == NX * NZ - 1
    at_first_y, at_last_y = me_y == 0, me_y == side_y - 1
    edges = (
        (0, (gx_back, me_y)),
        (1, (gx_next, me_y)),
        (2, (me_x, gy_back)),
        (3, (me_x, gy_next)),
        (1, (gx_next, gy_back)),
        (0, (gx_back, gy_next)),
    )

    def remote(src, dst, send, recv, device):
        return pltpu.make_async_remote_copy(
            src_ref=src, dst_ref=dst, send_sem=send, recv_sem=recv, device_id=device, device_id_type=MESH
        )

    def rows(c):
        return pl.ds(pl.multiple_of(c * ROWS, ROWS), ROWS)

    def own_load(c):
        return pltpu.make_async_copy(obs_ref.at[:, rows(c), :], ag.at[0, c], own_sem.at[c])

    def own_send(side, c):
        return remote(
            obs_ref.at[:, rows(c), :], ag.at[1 + side, c], ag_s.at[side, c], ag_r.at[side, c],
            (x_right, x_left)[side],
        )

    def far_send(side, c):
        piece = pl.ds(side * half, half)
        return remote(
            ag.at[1 + side, c, piece], ag.at[3, c, piece], ag_s.at[2 + side, c], ag_r.at[2 + side, c],
            (x_right, x_left)[side],
        )

    def meta_send(peer):
        return remote(
            meta_ref, meta.at[peer], meta_s.at[peer], meta_r.at[peer], (x_right, x_left, x_far)[peer]
        )

    def ring_send(side, stage, c):
        device = (z_right, z_left)[side]
        semaphores = (rs_s.at[side * 4 + stage - 1, c], rs_r.at[side * 4 + stage - 1, c])
        if stage == 1:
            return remote(
                part.at[c, 4, pl.ds(side * 2, 2)], (rp1, rm1)[side].at[c], *semaphores, device
            )
        source = 5 - stage if side == 0 else 3 + stage
        return remote(part.at[c, source], (rp, rm)[side].at[stage - 2, c], *semaphores, device)

    def ring_send_w(side, stage):
        source = 5 - stage if side == 0 else (8 if stage == 1 else 3 + stage)
        index = side * 4 + stage - 1
        return remote(
            part_w.at[source], rw.at[index], rw_s.at[index], rw_r.at[index], (z_right, z_left)[side]
        )

    def edge_send(e, place):
        message, device = edges[place]
        return remote(
            edge.at[e, message], halo.at[e, place], edge_s.at[e, place], edge_r.at[e, place], device
        )

    barrier = pltpu.get_barrier_semaphore()
    for device in (x_right, x_left, x_far, z_right, z_left, *(device for _, device in edges)):
        pl.semaphore_signal(barrier, inc=1, device_id=device, device_id_type=MESH)
    pairs = (
        (owner_in, owner_ref), (slot_in, slot_ref), (weight_in, weight_ref), (vel_in, vel_ref),
        (visc_in, visc_ref), (fric_in, fric_ref), (drive_in, drive_ref), (ice_in, ice_ref),
    )
    loads = [pltpu.make_async_copy(a, b, load_sem.at[n]) for n, (a, b) in enumerate(pairs)]
    for load in loads:
        load.start()
    for c in range(chunks):
        own_load(c).start()
    for load in loads[:3]:
        load.wait()
    key = (owner_ref[...] * SLOTS + slot_ref[...]).astype(jnp.float32)
    place = lax.broadcasted_iota(jnp.int32, (scenes, scenes), 0)
    same = place == lax.broadcasted_iota(jnp.int32, (scenes, scenes), 1)
    spread = lax.broadcasted_iota(jnp.int32, (scenes, scenes * ROWS), 1) // ROWS
    spread = spread == lax.broadcasted_iota(jnp.int32, (scenes, scenes * ROWS), 0)
    for r, value in enumerate((key, weight_ref[...].astype(jnp.float32))):
        column = jnp.sum(jnp.where(same, value, 0.0), axis=1, keepdims=True)
        meta_ref[r : r + 1, :] = jnp.sum(jnp.where(spread, column, 0.0), axis=0, keepdims=True)
    pl.semaphore_wait(barrier, 11)

    for peer in range(3):
        meta_send(peer).start()
    for c in range(LEAD):
        own_send(0, c).start()
        own_send(1, c).start()

    cells = visc_ref.shape[0]
    row_of = lax.broadcasted_iota(jnp.int32, (cells, 1), 0)
    lane_of = lax.broadcasted_iota(jnp.int32, (1, cells), 1)

    def send_edges(e, u, v, visc=None):
        edge[e, 0, 0:1, :] = u[0:1, :]
        edge[e, 0, 1:2, :] = v[0:1, :]
        edge[e, 1, 0:1, :] = u[cells - 1 :, :]
        edge[e, 1, 1:2, :] = v[cells - 1 :, :]
        lane = lane_of[:, :128]
        packed = jnp.where(lane == 0, u[:, :128], pltpu.roll(v[:, :128], 1, 1))
        packed = jnp.where(lane == 2, pltpu.roll(u[:, cells - 128 :], 3, 1), packed)
        packed = jnp.where(lane == 3, pltpu.roll(v[:, cells - 128 :], 4, 1), packed)
        if visc is not None:
            edge[e, 1, 2:3, :] = visc[cells - 1 :, :]
            packed = jnp.where(lane == 4, pltpu.roll(visc[:, cells - 128 :], 5, 1), packed)
        turned = packed.T
        edge[e, 2, 0:2, :] = turned[0:2]
        edge[e, 3, 0:3, :] = turned[2:5]
        for place in range(6):
            edge_send(e, place).start()

    def lower_x(field, row):
        return jnp.where(row_of == 0, row, pltpu.roll(field, 1, 0))

    def lower_y(field, column):
        return jnp.where(lane_of == 0, column, pltpu.roll(field, 1, 1))

    def stress_image(e, u, v, visc):
        for place in range(6):
            edge_send(e, place).wait_recv()

        def got(place, r):
            return halo[e, place, r : r + 1, :]

        zero = jnp.zeros((1, cells), jnp.float32)
        up_x = [jnp.where(at_last_x, zero, got(0, r)) for r in range(2)]
        up_y = [jnp.where(at_last_y, zero, got(2, r)) for r in range(2)]
        visc_x = jnp.where(at_first_x, zero, halo[0, 1, 2:3, :])
        visc_y = jnp.where(at_first_y, zero, halo[0, 3, 2:3, :])
        back_x = [got(1, r) for r in range(2)]
        back_y = [got(3, r) for r in range(2)]
        back_x_up, back_y_up = [], []
        for r in range(2):
            corner = jnp.where(at_last_y, 0.0, halo[e, 4, r : r + 1, 0:1])
            back_x_up.append(jnp.where(lane_of == cells - 1, corner, pltpu.roll(back_x[r], cells - 1, 1)))
            corner = jnp.where(at_last_x, 0.0, halo[e, 5, r : r + 1, cells - 1 : cells])
            back_y_up.append(jnp.where(lane_of == cells - 1, corner, pltpu.roll(back_y[r], cells - 1, 1)))
        sxx_x = visc_x * (4.0 * (u[0:1, :] - back_x[0]) + 2.0 * (back_x_up[1] - back_x[1]))
        sxy_x = visc_x * ((back_x_up[0] - back_x[0]) + (v[0:1, :] - back_x[1]))
        u_y, v_y = edge[e, 2, 0:1, :], edge[e, 2, 1:2, :]
        sxy_y = visc_y * ((u_y - back_y[0]) + (back_y_up[1] - back_y[1]))
        syy_y = visc_y * (4.0 * (v_y - back_y[1]) + 2.0 * (back_y_up[0] - back_y[0]))
        columns = jnp.concatenate([up_y[0], up_y[1], sxy_y, syy_y, visc_y, zero, zero, zero], axis=0).T
        column = [columns[:, r : r + 1] for r in range(5)]
        a_x = jnp.where(row_of == cells - 1, up_x[0], pltpu.roll(u, cells - 1, 0)) - u
        b_x = jnp.where(row_of == cells - 1, up_x[1], pltpu.roll(v, cells - 1, 0)) - v
        a_y = jnp.where(lane_of == cells - 1, column[0], pltpu.roll(u, cells - 1, 1)) - u
        b_y = jnp.where(lane_of == cells - 1, column[1], pltpu.roll(v, cells - 1, 1)) - v
        sxx = visc * (4.0 * a_x + 2.0 * b_y)
        syy = visc * (4.0 * b_y + 2.0 * a_x)
        sxy = visc * (a_y + b_x)
        push_u = lower_x(sxx, sxx_x) - sxx + lower_y(sxy, column[2]) - sxy
        push_v = lower_x(sxy, sxy_x) - sxy + lower_y(syy, column[3]) - syy
        return (push_u, push_v), visc_x, column[4]

    def first_sweep():
        visc, fric = visc_ref[...], fric_ref[...]
        start = [vel_ref[r].astype(jnp.float32) for r in range(2)]
        push, row, column = stress_image(0, start[0], start[1], visc)
        visc_x, visc_y = lower_x(visc, row), lower_y(visc, column)
        diag = (5.0 * visc + 4.0 * visc_x + visc_y, 5.0 * visc + visc_x + 4.0 * visc_y)
        for r in range(2):
            relax_r = 1.0 / (diag[r] + fric)
            relax[r] = relax_r
            moved = relax_r * (drive_ref[r].astype(jnp.float32) - push[r] - fric * start[r])
            q_one[r] = moved + start[r]
            first[r] = start[r] + OMEGA * moved
        send_edges(1, first[0], first[1])

    def second_sweep():
        fric = fric_ref[...]
        push, _, _ = stress_image(1, first[0], first[1], visc_ref[...])
        for r in range(2):
            moved = relax[r] * (drive_ref[r].astype(jnp.float32) - push[r] - fric * first[r])
            q_two[r] = moved + first[r]
            second[r] = first[r] + OMEGA * moved

    def adjoint():
        fric = fric_ref[...]
        u, v = lift[0], lift[1]
        send_edges(2, u, v)
        push, _, _ = stress_image(2, u, v, visc_ref[...])
        total = None
        for r in range(2):
            lift_one = OMEGA * relax[r] * (misfit[r] - push[r] - fric * lift[r])
            term = lift_one * q_one[r] + lift[r] * q_two[r]
            total = term if total is None else total + term
        tile = cells // 2
        for s in range(SLOTS):
            i, j = s // 2 * tile, s % 2 * tile
            out_ref[i : i + tile, j : j + tile] = -ice(s) * total[i : i + tile, j : j + tile]

    def ice(s):
        return ice_ref[s // 2, s % 2].astype(jnp.float32)

    width = scenes * ROWS
    count = NZ * SLOTS * ROWS

    def fill(source, block):
        key, weight = block[0:1, :], block[1:2, :]
        row = lax.broadcasted_iota(jnp.int32, (count, 1), 0)
        lane = lax.broadcasted_iota(jnp.int32, (1, width), 1)
        target_z = lax.rem(z + row // (SLOTS * ROWS), NZ)
        want = (target_z * NX + x) * SLOTS + lax.rem(row // ROWS, SLOTS)
        want = want.astype(jnp.float32)
        hit = jnp.logical_and(key == want, lax.rem(lane, ROWS) == lax.rem(row, ROWS))
        table[:, source * width : (source + 1) * width] = jnp.where(hit, weight, 0.0).astype(jnp.bfloat16)
        row = lax.broadcasted_iota(jnp.int32, (NZ * 8, 1), 0)
        slot = lax.rem(row, 8)
        target_z = lax.rem(z + row // 8, NZ)
        want = jnp.where(slot < SLOTS, (target_z * NX + x) * SLOTS + slot, -1).astype(jnp.float32)
        hit = jnp.logical_and(key == want, lax.rem(lane, ROWS) == 0)
        return jnp.sum(jnp.where(hit, weight, 0.0), axis=1, keepdims=True)

    total_w = fill(0, meta_ref[...])
    for peer in range(3):
        meta_send(peer).wait_recv()
        total_w = total_w + fill(1 + peer, meta[peer])
    total_w = jnp.broadcast_to(total_w, (NZ * 8, 128)).reshape(NZ, 8, 128)
    part_w[0:NZ] = total_w
    slot = lax.broadcasted_iota(jnp.int32, (8, 128), 0)
    part_w[4] = jnp.where(slot < 2, total_w[4], 0.0)
    part_w[8] = jnp.where(slot < 2, 0.0, total_w[4])
    ring_send_w(0, 1).start()
    ring_send_w(1, 1).start()
    for c in range(chunks):
        own_load(c).wait()
    for load in loads[3:]:
        load.wait()
    send_edges(0, vel_ref[0].astype(jnp.float32), vel_ref[1].astype(jnp.float32), visc_ref[...])

    def at_chunk(c, action):
        pl.when(jnp.logical_and(c >= 0, c < chunks))(lambda: action(c))

    def combine(c):
        for side in range(2):
            far_send(side, c).wait_recv()
        columns = []
        for h in range(ROWS // 16):
            columns.append(
                jnp.concatenate(
                    [ag[s, c, :, h * 16 : (h + 1) * 16, :].reshape(scenes * 16, 128) for s in range(4)], axis=0
                )
            )
        stacked = columns[0] if len(columns) == 1 else jnp.concatenate(columns, axis=1)
        sums = jnp.dot(table[...], stacked, preferred_element_type=jnp.float32)
        part[c] = sums.reshape(NZ, SLOTS, ROWS, 128)
        ring_send(0, 1, c).start()
        ring_send(1, 1, c).start()

    def ring_step(stage, c):
        for side in range(2):
            ring_send(side, stage - 1, c).wait_recv()
            mine = 5 - stage if side == 0 else 3 + stage
            if stage == 2:
                part[c, mine, side * 2 : side * 2 + 2] += (rp1, rm1)[side][c]
            else:
                part[c, mine] += (rp, rm)[side][stage - 3, c]
            ring_send(side, stage, c).start()

    def finish(c):
        for side in range(2):
            ring_send(side, 4, c).wait_recv()
        obs_sum = part[c, 0] + (rp[2, c] + rm[2, c])
        tile = cells // 2
        component = c // (chunks // 2)
        offset = lax.rem(c, chunks // 2) * ROWS
        for s in range(SLOTS):
            at = (
                component,
                pl.ds(pl.multiple_of(s // 2 * tile + offset, ROWS), ROWS),
                slice(s % 2 * tile, s % 2 * tile + tile),
            )
            value = ice(s) * (part_w[0, s : s + 1, :] * second[at] - obs_sum[s])
            misfit[at] = value
            lift[at] = OMEGA * relax[at] * value

    def ring_step_w(stage):
        for side in range(2):
            ring_send_w(side, stage - 1).wait_recv()
            mine = 5 - stage if side == 0 else 3 + stage
            part_w[mine] += rw[side * 4 + stage - 2]
            ring_send_w(side, stage).start()

    def finish_w():
        for side in range(2):
            ring_send_w(side, 4).wait_recv()
        part_w[0] += rw[3] + rw[7]

    def step(k, carry):
        @pl.when(k + LEAD < chunks)
        def _():
            own_send(0, k + LEAD).start()
            own_send(1, k + LEAD).start()

        @pl.when(k < chunks)
        def _():
            for side in range(2):
                own_send(side, k).wait_recv()
                far_send(side, k).start()

        pl.when(k == 1 + 4 * GAP)(finish_w)
        at_chunk(k - 1 - 4 * GAP, finish)
        for stage in (4, 3, 2):
            at_chunk(k - 1 - (stage - 1) * GAP, functools.partial(ring_step, stage))
            pl.when(k == stage - 1)(functools.partial(ring_step_w, stage))
        at_chunk(k - 1, combine)
        pl.when(k == 1)(first_sweep)
        pl.when(k == 3)(second_sweep)
        return carry

    lax.fori_loop(0, chunks + 1 + 4 * GAP, step, 0)
    adjoint()

    def drain(c, carry):
        for side in range(2):
            own_send(side, c).wait_send()
            far_send(side, c).wait_send()
            for stage in range(1, 5):
                ring_send(side, stage, c).wait_send()
        return carry

    lax.fori_loop(0, chunks, drain, 0)
    for peer in range(3):
        meta_send(peer).wait_send()
    for side in range(2):
        for stage in range(1, 5):
            ring_send_w(side, stage).wait_send()
    for e in range(3):
        for place in range(6):
            edge_send(e, place).wait_send()


def body(vel0, visc, fric, drive, scene_obs, scene_weight, scene_owner, scene_slot, ice_mask):
    obs = scene_obs[0]
    cells = visc.shape[0]
    scenes, _, tile, _ = obs.shape
    height = 2 * tile
    chunks = height // ROWS
    f32, bf16 = jnp.float32, jnp.bfloat16
    dma = pltpu.SemaphoreType.DMA
    return pl.pallas_call(
        exchange_kernel,
        out_shape=jax.ShapeDtypeStruct((cells, cells), f32),
        in_specs=[
            pl.BlockSpec(memory_space=pltpu.HBM)
        ] * 9,
        out_specs=pl.BlockSpec(memory_space=pltpu.VMEM),
        scratch_shapes=[
            pltpu.VMEM((1, scenes), jnp.int32),
            pltpu.VMEM((1, scenes), jnp.int32),
            pltpu.VMEM((1, scenes), bf16),
            pltpu.SMEM((2, 2), jnp.int32),
            pltpu.VMEM((2, cells, cells), bf16),
            pltpu.VMEM((cells, cells), f32),
            pltpu.VMEM((cells, cells), f32),
            pltpu.VMEM((2, cells, cells), bf16),
            pltpu.VMEM((8, scenes * ROWS), f32),
            *[pltpu.VMEM((2, cells, cells), f32)] * 7,
            pltpu.VMEM((3, 4, 8, cells), f32),
            pltpu.VMEM((3, 6, 8, cells), f32),
            pltpu.VMEM((3, 8, scenes * ROWS), f32),
            pltpu.VMEM((4, chunks, scenes, ROWS, tile), bf16),
            pltpu.VMEM((NZ * SLOTS * ROWS, 4 * scenes * ROWS), bf16),
            pltpu.VMEM((chunks, NZ, SLOTS, ROWS, tile), f32),
            pltpu.VMEM((NZ + 1, 8, 128), f32),
            pltpu.VMEM((chunks, 2, ROWS, tile), f32),
            pltpu.VMEM((3, chunks, SLOTS, ROWS, tile), f32),
            pltpu.VMEM((chunks, 2, ROWS, tile), f32),
            pltpu.VMEM((3, chunks, SLOTS, ROWS, tile), f32),
            pltpu.VMEM((8, 8, 128), f32),
            dma((chunks,)),
            dma((3,)), dma((3,)),
            dma((4, chunks)), dma((4, chunks)),
            dma((8, chunks)), dma((8, chunks)),
            dma((8,)), dma((8,)),
            dma((3, 6)), dma((3, 6)),
            dma((8,)),
        ],
        compiler_params=pltpu.CompilerParams(
            collective_id=0, has_side_effects=True, vmem_limit_bytes=67043328
        ),
    )(scene_owner.reshape(1, scenes), scene_slot, scene_weight, ice_mask, vel0, visc, fric, drive, obs.reshape(scenes, height, tile))


def solution(mesh):
    placed = (
        P(None, "gx", "gy"),
        P("gx", "gy"),
        P("gx", "gy"),
        P(None, "gx", "gy"),
        P("gy", "gx", None, None, None),
        P("gy", "gx"),
        P("gy", "gx", None),
        P("gy", "gx"),
        P("gx", "gy"),
    )
    return jax.shard_map(body, mesh=mesh, in_specs=placed, out_specs=P("gx", "gy"), check_vma=False)
```

```python
import functools

import jax
import jax.numpy as jnp
from jax import lax
from jax.experimental import pallas as pl
from jax.experimental.pallas import tpu as pltpu
from jax.sharding import PartitionSpec as P

OMEGA = 0.6
NX, NZ = 4, 8
SLOTS = 4
STRIP = 32
ROWS = 16
LEAD = 3
GAP = 2
MESH = pl.DeviceIdType.MESH


def exchange_kernel(
    owner_in, slot_in, weight_in, ice_in, vel_in, visc_in, fric_in, drive_in, obs_ref, out_ref,
    owner_ref, slot_ref, weight_ref, ice_ref, vel_ref, visc_ref, fric_ref, drive_ref, meta_ref,
    relax, first, second, gain, q_two, misfit, lift, edge, halo, gain_edge,
    meta, ag, table, part, part_w, rp1, rp, rm1, rm, rw,
    own_sem, meta_s, meta_r, ag_s, ag_r, rs_s, rs_r, rw_s, rw_r, edge_s, edge_r, load_sem,
):
    chunks = ag.shape[1]
    scenes = ag.shape[2]
    half = scenes // 2
    me_x, me_y = lax.axis_index("gx"), lax.axis_index("gy")
    x, z = lax.rem(me_x, NX), me_x // NX
    x_right = (z * NX + lax.rem(x + 1, NX), me_y)
    x_left = (z * NX + lax.rem(x + NX - 1, NX), me_y)
    x_far = (z * NX + lax.rem(x + 2, NX), me_y)
    z_right = (lax.rem(z + 1, NZ) * NX + x, me_y)
    z_left = (lax.rem(z + NZ - 1, NZ) * NX + x, me_y)

    gx_next, gx_back = lax.rem(me_x + 1, NX * NZ), lax.rem(me_x + NX * NZ - 1, NX * NZ)
    side_y = lax.axis_size("gy")
    gy_next, gy_back = lax.rem(me_y + 1, side_y), lax.rem(me_y + side_y - 1, side_y)
    at_first_x, at_last_x = me_x == 0, me_x == NX * NZ - 1
    at_first_y, at_last_y = me_y == 0, me_y == side_y - 1
    edges = (
        (0, (gx_back, me_y)),
        (1, (gx_next, me_y)),
        (2, (me_x, gy_back)),
        (3, (me_x, gy_next)),
        (1, (gx_next, gy_back)),
        (0, (gx_back, gy_next)),
    )

    def remote(src, dst, send, recv, device):
        return pltpu.make_async_remote_copy(
            src_ref=src, dst_ref=dst, send_sem=send, recv_sem=recv, device_id=device, device_id_type=MESH
        )

    def rows(c):
        return pl.ds(pl.multiple_of(c * ROWS, ROWS), ROWS)

    def own_load(c):
        return pltpu.make_async_copy(obs_ref.at[:, rows(c), :], ag.at[0, c], own_sem.at[c])

    def own_send(side, c):
        return remote(
            obs_ref.at[:, rows(c), :], ag.at[1 + side, c], ag_s.at[side, c], ag_r.at[side, c],
            (x_right, x_left)[side],
        )

    def far_send(side, c):
        piece = pl.ds(side * half, half)
        return remote(
            ag.at[1 + side, c, piece], ag.at[3, c, piece], ag_s.at[2 + side, c], ag_r.at[2 + side, c],
            (x_right, x_left)[side],
        )

    def meta_send(peer):
        return remote(
            meta_ref, meta.at[peer], meta_s.at[peer], meta_r.at[peer], (x_right, x_left, x_far)[peer]
        )

    def ring_send(side, stage, c):
        device = (z_right, z_left)[side]
        semaphores = (rs_s.at[side * 4 + stage - 1, c], rs_r.at[side * 4 + stage - 1, c])
        if stage == 1:
            return remote(
                part.at[c, 4, pl.ds(side * 2, 2)], (rp1, rm1)[side].at[c], *semaphores, device
            )
        source = 5 - stage if side == 0 else 3 + stage
        return remote(part.at[c, source], (rp, rm)[side].at[stage - 2, c], *semaphores, device)

    def ring_send_w(side, stage):
        source = 5 - stage if side == 0 else (8 if stage == 1 else 3 + stage)
        index = side * 4 + stage - 1
        return remote(
            part_w.at[source], rw.at[index], rw_s.at[index], rw_r.at[index], (z_right, z_left)[side]
        )

    def edge_send(e, place):
        message, device = edges[place]
        return remote(
            edge.at[e, message], halo.at[e, place], edge_s.at[e, place], edge_r.at[e, place], device
        )

    barrier = pltpu.get_barrier_semaphore()
    for device in (x_right, x_left, x_far, z_right, z_left, *(device for _, device in edges)):
        pl.semaphore_signal(barrier, inc=1, device_id=device, device_id_type=MESH)
    pairs = (
        (owner_in, owner_ref), (slot_in, slot_ref), (weight_in, weight_ref), (vel_in, vel_ref),
        (visc_in, visc_ref), (fric_in, fric_ref), (drive_in, drive_ref), (ice_in, ice_ref),
    )
    loads = [pltpu.make_async_copy(a, b, load_sem.at[n]) for n, (a, b) in enumerate(pairs)]
    for load in loads:
        load.start()
    for c in range(chunks):
        own_load(c).start()
    for load in loads[:3]:
        load.wait()
    key = (owner_ref[...] * SLOTS + slot_ref[...]).astype(jnp.float32)
    place = lax.broadcasted_iota(jnp.int32, (scenes, scenes), 0)
    same = place == lax.broadcasted_iota(jnp.int32, (scenes, scenes), 1)
    spread = lax.broadcasted_iota(jnp.int32, (scenes, scenes * ROWS), 1) // ROWS
    spread = spread == lax.broadcasted_iota(jnp.int32, (scenes, scenes * ROWS), 0)
    for r, value in enumerate((key, weight_ref[...].astype(jnp.float32))):
        column = jnp.sum(jnp.where(same, value, 0.0), axis=1, keepdims=True)
        meta_ref[r : r + 1, :] = jnp.sum(jnp.where(spread, column, 0.0), axis=0, keepdims=True)
    pl.semaphore_wait(barrier, 11)

    for peer in range(3):
        meta_send(peer).start()
    for c in range(LEAD):
        own_send(0, c).start()
        own_send(1, c).start()

    cells = visc_ref.shape[0]
    lane_of = lax.broadcasted_iota(jnp.int32, (1, cells), 1)

    def columns_of(*columns):
        lane, packed = lane_of[:, :128], None
        for n, (last, array) in enumerate(columns):
            block = array[:, cells - 128 :] if last else array[:, :128]
            moved = (n + 1 if last else n) % 128
            block = pltpu.roll(block, moved, 1) if moved else block
            packed = block if packed is None else jnp.where(lane == n, block, packed)
        return packed.T

    def send_edges(e, u, v, visc=None):
        for r, array in enumerate((u, v)):
            edge[e, 0, r : r + 1, :] = array[0:1, :]
            edge[e, 1, r : r + 1, :] = array[cells - 1 :, :]
        columns = [(False, u), (False, v), (True, u), (True, v)]
        if visc is not None:
            edge[e, 1, 2:3, :] = visc[cells - 1 :, :]
            columns.append((True, visc))
        turned = columns_of(*columns)
        edge[e, 2, 0:2, :] = turned[0:2]
        edge[e, 3, 0:3, :] = turned[2:5]
        for place in range(6):
            edge_send(e, place).start()

    def outside(e, u_first, v_first):
        for place in range(6):
            edge_send(e, place).wait_recv()

        def got(place, r):
            return halo[e, place, r : r + 1, :]

        zero = jnp.zeros((1, cells), jnp.float32)
        up_x = [jnp.where(at_last_x, zero, got(0, r)) for r in range(2)]
        up_y = [jnp.where(at_last_y, zero, got(2, r)) for r in range(2)]
        visc_x = jnp.where(at_first_x, zero, halo[0, 1, 2:3, :])
        visc_y = jnp.where(at_first_y, zero, halo[0, 3, 2:3, :])
        back_x = [got(1, r) for r in range(2)]
        back_y = [got(3, r) for r in range(2)]
        back_x_up, back_y_up = [], []
        for r in range(2):
            corner = jnp.where(at_last_y, 0.0, halo[e, 4, r : r + 1, 0:1])
            back_x_up.append(jnp.where(lane_of == cells - 1, corner, pltpu.roll(back_x[r], cells - 1, 1)))
            corner = jnp.where(at_last_x, 0.0, halo[e, 5, r : r + 1, cells - 1 : cells])
            back_y_up.append(jnp.where(lane_of == cells - 1, corner, pltpu.roll(back_y[r], cells - 1, 1)))
        sxx_x = visc_x * (4.0 * (u_first - back_x[0]) + 2.0 * (back_x_up[1] - back_x[1]))
        sxy_x = visc_x * ((back_x_up[0] - back_x[0]) + (v_first - back_x[1]))
        u_y, v_y = edge[e, 2, 0:1, :], edge[e, 2, 1:2, :]
        sxy_y = visc_y * ((u_y - back_y[0]) + (back_y_up[1] - back_y[1]))
        syy_y = visc_y * (4.0 * (v_y - back_y[1]) + 2.0 * (back_y_up[0] - back_y[0]))
        return up_x, up_y, visc_x, visc_y, sxx_x, sxy_x, sxy_y, syy_y

    def as_columns(*rows):
        zero = jnp.zeros((8 - len(rows), cells), jnp.float32)
        turned = jnp.concatenate([*rows, zero], axis=0).T
        return [turned[:, n : n + 1] for n in range(len(rows))]

    strip_row = lax.broadcasted_iota(jnp.int32, (STRIP, 1), 0)

    def upper_x(field, row):
        return jnp.where(strip_row == STRIP - 1, row, pltpu.roll(field, STRIP - 1, 0))

    def lower_x(field, row):
        return jnp.where(strip_row == 0, row, pltpu.roll(field, 1, 0))

    def upper_y(field, column):
        return jnp.where(lane_of == cells - 1, column, pltpu.roll(field, cells - 1, 1))

    def lower_y(field, column):
        return jnp.where(lane_of == 0, column, pltpu.roll(field, 1, 1))

    def stress_images(field, up_x, up_y, sxx_x, sxy_x, sxy_y, syy_y, apply):
        for i in range(0, cells, STRIP):
            rows_i = slice(i, i + STRIP)
            u, v = field(0, rows_i), field(1, rows_i)
            following = slice(i + STRIP, i + STRIP + 1)
            after = up_x if i + STRIP == cells else [field(r, following) for r in range(2)]
            a_x, b_x = upper_x(u, after[0]) - u, upper_x(v, after[1]) - v
            a_y = upper_y(u, take(up_y[0], rows_i)) - u
            b_y = upper_y(v, take(up_y[1], rows_i)) - v
            visc = visc_ref[rows_i, :]
            sxx = visc * (4.0 * a_x + 2.0 * b_y)
            syy = visc * (4.0 * b_y + 2.0 * a_x)
            sxy = visc * (a_y + b_x)
            push_u = lower_x(sxx, sxx_x) - sxx + lower_y(sxy, take(sxy_y, rows_i)) - sxy
            push_v = lower_x(sxy, sxy_x) - sxy + lower_y(syy, take(syy_y, rows_i)) - syy
            apply(rows_i, (u, v), (push_u, push_v))
            sxx_x, sxy_x = sxx[STRIP - 1 :, :], sxy[STRIP - 1 :, :]

    def take(column, rows_i):
        return column if isinstance(column, float) else column[rows_i, :]

    def ice_row(rows_i):
        s = rows_i.start // (cells // 2) * 2
        return jnp.where(lane_of < cells // 2, ice(s), ice(s + 1))

    def first_sweep():
        def field(r, rows_i):
            return vel_ref[r, rows_i, :].astype(jnp.float32)

        up_x, up_y, visc_x, visc_y, sxx_x, sxy_x, sxy_y, syy_y = outside(0, field(0, slice(0, 1)), field(1, slice(0, 1)))
        *columns, visc_y = as_columns(up_y[0], up_y[1], sxy_y, syy_y, visc_y)

        def apply(rows_i, start, push):
            visc, fric = visc_ref[rows_i, :], fric_ref[rows_i, :]
            before = visc_x if rows_i.start == 0 else visc_ref[rows_i.start - 1 : rows_i.start, :]
            behind_x, behind_y = lower_x(visc, before), lower_y(visc, visc_y[rows_i, :])
            diag = (5.0 * visc + 4.0 * behind_x + behind_y, 5.0 * visc + behind_x + 4.0 * behind_y)
            for r in range(2):
                relax_r = 1.0 / (diag[r] + fric)
                relax[r, rows_i, :] = OMEGA * relax_r
                moved = relax_r * (drive_ref[r, rows_i, :].astype(jnp.float32) - push[r] - fric * start[r])
                gain[r, rows_i, :] = ice_row(rows_i) * (OMEGA * relax_r) * (moved + start[r])
                first[r, rows_i, :] = start[r] + OMEGA * moved

        stress_images(field, up_x, columns[:2], sxx_x, sxy_x, columns[2], columns[3], apply)
        send_edges(1, first.at[0], first.at[1])

    def second_sweep():
        def field(r, rows_i):
            return first[r, rows_i, :]

        up_x, up_y, _, _, sxx_x, sxy_x, sxy_y, syy_y = outside(1, field(0, slice(0, 1)), field(1, slice(0, 1)))
        columns = as_columns(up_y[0], up_y[1], sxy_y, syy_y)

        def apply(rows_i, start, push):
            fric = fric_ref[rows_i, :]
            for r in range(2):
                residual = drive_ref[r, rows_i, :].astype(jnp.float32) - push[r] - fric * start[r]
                moved = relax[r, rows_i, :] * residual
                q_two[r, rows_i, :] = ice_row(rows_i) * ((1.0 / OMEGA) * moved + start[r])
                second[r, rows_i, :] = start[r] + moved

        stress_images(field, up_x, columns[:2], sxx_x, sxy_x, columns[2], columns[3], apply)
        gains = columns_of((False, gain.at[0]), (False, gain.at[1]), (True, gain.at[0]), (True, gain.at[1]))
        gain_edge[0:4, :] = gains[0:4]

    def adjoint():
        def field(r, rows_i):
            return lift[r, rows_i, :]

        send_edges(2, lift.at[0], lift.at[1])

        def apply(rows_i, lifted, push):
            fric = fric_ref[rows_i, :]
            total = None
            for r in range(2):
                back = push[r] - misfit[r, rows_i, :] + fric * lifted[r]
                term = gain[r, rows_i, :] * back - q_two[r, rows_i, :] * lifted[r]
                total = term if total is None else total + term
            out_ref[rows_i, :] = total

        zero = jnp.zeros((1, cells), jnp.float32)
        stress_images(field, (zero, zero), (0.0, 0.0), zero, zero, 0.0, 0.0, apply)
        up_x, up_y, _, _, sxx_x, sxy_x, sxy_y, syy_y = outside(2, field(0, slice(0, 1)), field(1, slice(0, 1)))
        end = slice(cells - 1, cells)
        visc = visc_ref[end, :]
        sxx, syy, sxy = 4.0 * visc * up_x[0], 2.0 * visc * up_x[0], visc * up_x[1]
        push_u = lower_y(sxy, 0.0) - sxy - sxx
        push_v = lower_y(syy, 0.0) - syy - sxy
        out_ref[0:1, :] += gain[0, 0:1, :] * sxx_x + gain[1, 0:1, :] * sxy_x
        out_ref[end, :] += gain[0, end, :] * push_u + gain[1, end, :] * push_v
        visc = edge[0, 3, 2:3, :]
        sxx, syy, sxy = 2.0 * visc * up_y[1], 4.0 * visc * up_y[1], visc * up_y[0]
        push_u = lower_y(sxx, 0.0) - sxx - sxy
        push_v = lower_y(sxy, 0.0) - sxy - syy
        column_first, column_last = as_columns(
            gain_edge[0:1, :] * sxy_y + gain_edge[1:2, :] * syy_y,
            gain_edge[2:3, :] * push_u + gain_edge[3:4, :] * push_v,
        )
        lane = lane_of[:, :128]
        out_ref[:, :128] += jnp.where(lane == 0, column_first, 0.0)
        out_ref[:, cells - 128 :] += jnp.where(lane == 127, column_last, 0.0)

    def ice(s):
        return ice_ref[s // 2, s % 2].astype(jnp.float32)

    width = scenes * ROWS
    diagonal = lax.broadcasted_iota(jnp.int32, (ROWS, width), 0) == lax.bitwise_and(
        lax.broadcasted_iota(jnp.int32, (ROWS, width), 1), ROWS - 1
    )

    def fill(source, block):
        key, weight = block[0:1, :], block[1:2, :]
        for distance in range(NZ):
            owner = lax.rem(z + distance, NZ) * NX + x
            for slot in range(SLOTS):
                want = (owner * SLOTS + slot).astype(jnp.float32)
                chosen = jnp.where(key == want, weight, 0.0)
                at = (distance * SLOTS + slot) * ROWS
                table[at : at + ROWS, source * width : (source + 1) * width] = jnp.where(
                    diagonal, chosen, 0.0
                ).astype(jnp.bfloat16)

    for load in loads[3:]:
        load.wait()
    send_edges(0, vel_ref[0].astype(jnp.float32), vel_ref[1].astype(jnp.float32), visc_ref)
    fill(0, meta_ref[...])
    for peer in range(3):
        meta_send(peer).wait_recv()
        fill(1 + peer, meta[peer])
    ones = jnp.ones((4 * width, 128), jnp.bfloat16)
    total_w = jnp.dot(table[...], ones, preferred_element_type=jnp.float32)
    part_w[...] = jnp.zeros_like(part_w)
    for distance in range(NZ):
        for slot in range(SLOTS):
            at = (distance * SLOTS + slot) * ROWS
            place = NZ if distance == NZ // 2 and slot >= 2 else distance
            part_w[place, slot : slot + 1, :] = total_w[at : at + 1, :]
    ring_send_w(0, 1).start()
    ring_send_w(1, 1).start()
    for c in range(chunks):
        own_load(c).wait()
    def at_chunk(c, action):
        pl.when(jnp.logical_and(c >= 0, c < chunks))(lambda: action(c))

    def combine(c):
        for side in range(2):
            far_send(side, c).wait_recv()
        columns = []
        for h in range(ROWS // 16):
            columns.append(
                jnp.concatenate(
                    [ag[s, c, :, h * 16 : (h + 1) * 16, :].reshape(scenes * 16, 128) for s in range(4)], axis=0
                )
            )
        stacked = columns[0] if len(columns) == 1 else jnp.concatenate(columns, axis=1)
        sums = jnp.dot(table[...], stacked, preferred_element_type=jnp.float32)
        part[c] = sums.reshape(NZ, SLOTS, ROWS, 128)
        ring_send(0, 1, c).start()
        ring_send(1, 1, c).start()

    def ring_step(stage, c):
        for side in range(2):
            ring_send(side, stage - 1, c).wait_recv()
            mine = 5 - stage if side == 0 else 3 + stage
            if stage == 2:
                part[c, mine, side * 2 : side * 2 + 2] += (rp1, rm1)[side][c]
            else:
                part[c, mine] += (rp, rm)[side][stage - 3, c]
            ring_send(side, stage, c).start()

    def finish(c):
        for side in range(2):
            ring_send(side, 4, c).wait_recv()
        obs_sum = part[c, 0] + (rp[2, c] + rm[2, c])
        tile = cells // 2
        component = c // (chunks // 2)
        offset = lax.rem(c, chunks // 2) * ROWS
        for s in range(SLOTS):
            at = (
                component,
                pl.ds(pl.multiple_of(s // 2 * tile + offset, ROWS), ROWS),
                slice(s % 2 * tile, s % 2 * tile + tile),
            )
            value = ice(s) * (part_w[0, s : s + 1, :] * second[at] - obs_sum[s])
            misfit[at] = value
            lift[at] = relax[at] * value

    def ring_step_w(stage):
        for side in range(2):
            ring_send_w(side, stage - 1).wait_recv()
            mine = 5 - stage if side == 0 else 3 + stage
            part_w[mine] += rw[side * 4 + stage - 2]
            ring_send_w(side, stage).start()

    def finish_w():
        for side in range(2):
            ring_send_w(side, 4).wait_recv()
        part_w[0] += rw[3] + rw[7]

    def step(k, carry):
        @pl.when(k + LEAD < chunks)
        def _():
            own_send(0, k + LEAD).start()
            own_send(1, k + LEAD).start()

        @pl.when(k < chunks)
        def _():
            for side in range(2):
                own_send(side, k).wait_recv()
                far_send(side, k).start()

        pl.when(k == 1 + 4 * GAP)(finish_w)
        at_chunk(k - 1 - 4 * GAP, finish)
        for stage in (4, 3, 2):
            at_chunk(k - 1 - (stage - 1) * GAP, functools.partial(ring_step, stage))
            pl.when(k == 2 * stage - 3)(functools.partial(ring_step_w, stage))
        at_chunk(k - 1, combine)
        pl.when(k == 0)(first_sweep)
        pl.when(k == 2)(second_sweep)
        return carry

    lax.fori_loop(0, chunks + 1 + 4 * GAP, step, 0)
    adjoint()

    def drain(c, carry):
        for side in range(2):
            own_send(side, c).wait_send()
            far_send(side, c).wait_send()
            for stage in range(1, 5):
                ring_send(side, stage, c).wait_send()
        return carry

    lax.fori_loop(0, chunks, drain, 0)
    for peer in range(3):
        meta_send(peer).wait_send()
    for side in range(2):
        for stage in range(1, 5):
            ring_send_w(side, stage).wait_send()
    for e in range(3):
        for place in range(6):
            edge_send(e, place).wait_send()


def body(vel0, visc, fric, drive, scene_obs, scene_weight, scene_owner, scene_slot, ice_mask):
    obs = scene_obs[0]
    cells = visc.shape[0]
    scenes, _, tile, _ = obs.shape
    height = 2 * tile
    chunks = height // ROWS
    f32, bf16 = jnp.float32, jnp.bfloat16
    dma = pltpu.SemaphoreType.DMA
    return pl.pallas_call(
        exchange_kernel,
        out_shape=jax.ShapeDtypeStruct((cells, cells), f32),
        in_specs=[
            pl.BlockSpec(memory_space=pltpu.HBM)
        ] * 9,
        out_specs=pl.BlockSpec(memory_space=pltpu.VMEM),
        scratch_shapes=[
            pltpu.VMEM((1, scenes), jnp.int32),
            pltpu.VMEM((1, scenes), jnp.int32),
            pltpu.VMEM((1, scenes), bf16),
            pltpu.SMEM((2, 2), jnp.int32),
            pltpu.VMEM((2, cells, cells), bf16),
            pltpu.VMEM((cells, cells), f32),
            pltpu.VMEM((cells, cells), f32),
            pltpu.VMEM((2, cells, cells), bf16),
            pltpu.VMEM((8, scenes * ROWS), f32),
            *[pltpu.VMEM((2, cells, cells), f32)] * 7,
            pltpu.VMEM((3, 4, 8, cells), f32),
            pltpu.VMEM((3, 6, 8, cells), f32),
            pltpu.VMEM((8, cells), f32),
            pltpu.VMEM((3, 8, scenes * ROWS), f32),
            pltpu.VMEM((4, chunks, scenes, ROWS, tile), bf16),
            pltpu.VMEM((NZ * SLOTS * ROWS, 4 * scenes * ROWS), bf16),
            pltpu.VMEM((chunks, NZ, SLOTS, ROWS, tile), f32),
            pltpu.VMEM((NZ + 1, 8, 128), f32),
            pltpu.VMEM((chunks, 2, ROWS, tile), f32),
            pltpu.VMEM((3, chunks, SLOTS, ROWS, tile), f32),
            pltpu.VMEM((chunks, 2, ROWS, tile), f32),
            pltpu.VMEM((3, chunks, SLOTS, ROWS, tile), f32),
            pltpu.VMEM((8, 8, 128), f32),
            dma((chunks,)),
            dma((3,)), dma((3,)),
            dma((4, chunks)), dma((4, chunks)),
            dma((8, chunks)), dma((8, chunks)),
            dma((8,)), dma((8,)),
            dma((3, 6)), dma((3, 6)),
            dma((8,)),
        ],
        compiler_params=pltpu.CompilerParams(
            collective_id=0, has_side_effects=True, vmem_limit_bytes=67043328
        ),
    )(scene_owner.reshape(1, scenes), scene_slot, scene_weight, ice_mask, vel0, visc, fric, drive, obs.reshape(scenes, height, tile))


def solution(mesh):
    placed = (
        P(None, "gx", "gy"),
        P("gx", "gy"),
        P("gx", "gy"),
        P(None, "gx", "gy"),
        P("gy", "gx", None, None, None),
        P("gy", "gx"),
        P("gy", "gx", None),
        P("gy", "gx"),
        P("gx", "gy"),
    )
    return jax.shard_map(body, mesh=mesh, in_specs=placed, out_specs=P("gx", "gy"), check_vma=False)
```

```python
import functools

import jax
import jax.numpy as jnp
from jax import lax
from jax.experimental import pallas as pl
from jax.experimental.pallas import tpu as pltpu
from jax.sharding import PartitionSpec as P

OMEGA = 0.6
NX, NZ = 4, 8
SLOTS = 4
STRIP = 32
ROWS = 16
LEAD = 3
GAP = 2
MESH = pl.DeviceIdType.MESH


def exchange_kernel(
    owner_in, slot_in, weight_in, ice_in, vel_in, visc_in, fric_in, drive_in, obs_ref, out_ref,
    owner_ref, slot_ref, weight_ref, ice_ref, vel_ref, visc_ref, fric_ref, drive_ref, meta_ref,
    relax, first, second, gain, q_two, misfit, lift, edge, halo, gain_edge,
    meta, ag, table, part, part_w, rp1, rp, rm1, rm, rw,
    own_sem, meta_s, meta_r, ag_s, ag_r, rs_s, rs_r, rw_s, rw_r, edge_s, edge_r, load_sem,
):
    chunks = ag.shape[1]
    scenes = ag.shape[2]
    half = scenes // 2
    me_x, me_y = lax.axis_index("gx"), lax.axis_index("gy")
    x, z = lax.rem(me_x, NX), me_x // NX
    x_right = (z * NX + lax.rem(x + 1, NX), me_y)
    x_left = (z * NX + lax.rem(x + NX - 1, NX), me_y)
    x_far = (z * NX + lax.rem(x + 2, NX), me_y)
    z_right = (lax.rem(z + 1, NZ) * NX + x, me_y)
    z_left = (lax.rem(z + NZ - 1, NZ) * NX + x, me_y)

    gx_next, gx_back = lax.rem(me_x + 1, NX * NZ), lax.rem(me_x + NX * NZ - 1, NX * NZ)
    side_y = lax.axis_size("gy")
    gy_next, gy_back = lax.rem(me_y + 1, side_y), lax.rem(me_y + side_y - 1, side_y)
    at_first_x, at_last_x = me_x == 0, me_x == NX * NZ - 1
    at_first_y, at_last_y = me_y == 0, me_y == side_y - 1
    edges = (
        (0, (gx_back, me_y)),
        (1, (gx_next, me_y)),
        (2, (me_x, gy_back)),
        (3, (me_x, gy_next)),
        (1, (gx_next, gy_back)),
        (0, (gx_back, gy_next)),
    )

    def remote(src, dst, send, recv, device):
        return pltpu.make_async_remote_copy(
            src_ref=src, dst_ref=dst, send_sem=send, recv_sem=recv, device_id=device, device_id_type=MESH
        )

    def rows(c):
        return pl.ds(pl.multiple_of(c * ROWS, ROWS), ROWS)

    def own_load(c):
        return pltpu.make_async_copy(obs_ref.at[:, rows(c), :], ag.at[0, c], own_sem.at[c])

    def own_send(side, c):
        return remote(
            obs_ref.at[:, rows(c), :], ag.at[1 + side, c], ag_s.at[side, c], ag_r.at[side, c],
            (x_right, x_left)[side],
        )

    def far_send(side, c):
        piece = pl.ds(side * half, half)
        return remote(
            ag.at[1 + side, c, piece], ag.at[3, c, piece], ag_s.at[2 + side, c], ag_r.at[2 + side, c],
            (x_right, x_left)[side],
        )

    def meta_send(peer):
        return remote(
            meta_ref, meta.at[peer], meta_s.at[peer], meta_r.at[peer], (x_right, x_left, x_far)[peer]
        )

    def ring_send(side, stage, c):
        device = (z_right, z_left)[side]
        semaphores = (rs_s.at[side * 4 + stage - 1, c], rs_r.at[side * 4 + stage - 1, c])
        if stage == 1:
            return remote(
                part.at[c, 4, pl.ds(side * 2, 2)], (rp1, rm1)[side].at[c], *semaphores, device
            )
        source = 5 - stage if side == 0 else 3 + stage
        return remote(part.at[c, source], (rp, rm)[side].at[stage - 2, c], *semaphores, device)

    def ring_send_w(side, stage):
        source = 5 - stage if side == 0 else (8 if stage == 1 else 3 + stage)
        index = side * 4 + stage - 1
        return remote(
            part_w.at[source], rw.at[index], rw_s.at[index], rw_r.at[index], (z_right, z_left)[side]
        )

    def edge_send(e, place):
        message, device = edges[place]
        return remote(
            edge.at[e, message], halo.at[e, place], edge_s.at[e, place], edge_r.at[e, place], device
        )

    barrier = pltpu.get_barrier_semaphore()
    for device in (x_right, x_left, x_far, z_right, z_left, *(device for _, device in edges)):
        pl.semaphore_signal(barrier, inc=1, device_id=device, device_id_type=MESH)
    pairs = (
        (owner_in, owner_ref), (slot_in, slot_ref), (weight_in, weight_ref), (vel_in, vel_ref),
        (visc_in, visc_ref), (fric_in, fric_ref), (drive_in, drive_ref), (ice_in, ice_ref),
    )
    loads = [pltpu.make_async_copy(a, b, load_sem.at[n]) for n, (a, b) in enumerate(pairs)]
    for load in loads:
        load.start()
    for c in range(chunks):
        own_load(c).start()
    for load in loads[:3]:
        load.wait()
    key = (owner_ref[...] * SLOTS + slot_ref[...]).astype(jnp.float32)
    place = lax.broadcasted_iota(jnp.int32, (scenes, scenes), 0)
    same = place == lax.broadcasted_iota(jnp.int32, (scenes, scenes), 1)
    spread = lax.broadcasted_iota(jnp.int32, (scenes, scenes * ROWS), 1) // ROWS
    spread = spread == lax.broadcasted_iota(jnp.int32, (scenes, scenes * ROWS), 0)
    for r, value in enumerate((key, weight_ref[...].astype(jnp.float32))):
        column = jnp.sum(jnp.where(same, value, 0.0), axis=1, keepdims=True)
        meta_ref[r : r + 1, :] = jnp.sum(jnp.where(spread, column, 0.0), axis=0, keepdims=True)
    pl.semaphore_wait(barrier, 11)

    for peer in range(3):
        meta_send(peer).start()
    for c in range(LEAD):
        own_send(0, c).start()
        own_send(1, c).start()

    cells = visc_ref.shape[0]
    lane_of = lax.broadcasted_iota(jnp.int32, (1, cells), 1)

    def columns_of(*columns):
        lane, packed = lane_of[:, :128], None
        for n, (last, array) in enumerate(columns):
            block = array[:, cells - 128 :] if last else array[:, :128]
            moved = (n + 1 if last else n) % 128
            block = pltpu.roll(block, moved, 1) if moved else block
            packed = block if packed is None else jnp.where(lane == n, block, packed)
        return packed.T

    def send_edges(e, u, v, visc=None):
        for r, array in enumerate((u, v)):
            edge[e, 0, r : r + 1, :] = array[0:1, :]
            edge[e, 1, r : r + 1, :] = array[cells - 1 :, :]
        columns = [(False, u), (False, v), (True, u), (True, v)]
        if visc is not None:
            edge[e, 1, 2:3, :] = visc[cells - 1 :, :]
            columns.append((True, visc))
        turned = columns_of(*columns)
        edge[e, 2, 0:2, :] = turned[0:2]
        edge[e, 3, 0:3, :] = turned[2:5]
        for place in range(6):
            edge_send(e, place).start()

    def outside(e, u_first, v_first):
        for place in range(6):
            edge_send(e, place).wait_recv()

        def got(place, r):
            return halo[e, place, r : r + 1, :]

        zero = jnp.zeros((1, cells), jnp.float32)
        up_x = [jnp.where(at_last_x, zero, got(0, r)) for r in range(2)]
        up_y = [jnp.where(at_last_y, zero, got(2, r)) for r in range(2)]
        visc_x = jnp.where(at_first_x, zero, halo[0, 1, 2:3, :])
        visc_y = jnp.where(at_first_y, zero, halo[0, 3, 2:3, :])
        back_x = [got(1, r) for r in range(2)]
        back_y = [got(3, r) for r in range(2)]
        back_x_up, back_y_up = [], []
        for r in range(2):
            corner = jnp.where(at_last_y, 0.0, halo[e, 4, r : r + 1, 0:1])
            back_x_up.append(jnp.where(lane_of == cells - 1, corner, pltpu.roll(back_x[r], cells - 1, 1)))
            corner = jnp.where(at_last_x, 0.0, halo[e, 5, r : r + 1, cells - 1 : cells])
            back_y_up.append(jnp.where(lane_of == cells - 1, corner, pltpu.roll(back_y[r], cells - 1, 1)))
        sxx_x = visc_x * (4.0 * (u_first - back_x[0]) + 2.0 * (back_x_up[1] - back_x[1]))
        sxy_x = visc_x * ((back_x_up[0] - back_x[0]) + (v_first - back_x[1]))
        u_y, v_y = edge[e, 2, 0:1, :], edge[e, 2, 1:2, :]
        sxy_y = visc_y * ((u_y - back_y[0]) + (back_y_up[1] - back_y[1]))
        syy_y = visc_y * (4.0 * (v_y - back_y[1]) + 2.0 * (back_y_up[0] - back_y[0]))
        return up_x, up_y, visc_x, visc_y, sxx_x, sxy_x, sxy_y, syy_y

    def as_columns(*rows):
        zero = jnp.zeros((8 - len(rows), cells), jnp.float32)
        turned = jnp.concatenate([*rows, zero], axis=0).T
        return [turned[:, n : n + 1] for n in range(len(rows))]

    strip_row = lax.broadcasted_iota(jnp.int32, (STRIP, 1), 0)

    def upper_x(field, row):
        return jnp.where(strip_row == STRIP - 1, row, pltpu.roll(field, STRIP - 1, 0))

    def lower_x(field, row):
        return jnp.where(strip_row == 0, row, pltpu.roll(field, 1, 0))

    def upper_y(field, column):
        return jnp.where(lane_of == cells - 1, column, pltpu.roll(field, cells - 1, 1))

    def lower_y(field, column):
        return jnp.where(lane_of == 0, column, pltpu.roll(field, 1, 1))

    def stress_images(field, up_x, up_y, sxx_x, sxy_x, sxy_y, syy_y, apply):
        for i in range(0, cells, STRIP):
            rows_i = slice(i, i + STRIP)
            u, v = field(0, rows_i), field(1, rows_i)
            following = slice(i + STRIP, i + STRIP + 1)
            after = up_x if i + STRIP == cells else [field(r, following) for r in range(2)]
            a_x, b_x = upper_x(u, after[0]) - u, upper_x(v, after[1]) - v
            a_y = upper_y(u, take(up_y[0], rows_i)) - u
            b_y = upper_y(v, take(up_y[1], rows_i)) - v
            visc = visc_ref[rows_i, :]
            sxx = visc * (4.0 * a_x + 2.0 * b_y)
            syy = visc * (4.0 * b_y + 2.0 * a_x)
            sxy = visc * (a_y + b_x)
            push_u = lower_x(sxx, sxx_x) - sxx + lower_y(sxy, take(sxy_y, rows_i)) - sxy
            push_v = lower_x(sxy, sxy_x) - sxy + lower_y(syy, take(syy_y, rows_i)) - syy
            apply(rows_i, (u, v), (push_u, push_v))
            sxx_x, sxy_x = sxx[STRIP - 1 :, :], sxy[STRIP - 1 :, :]

    def take(column, rows_i):
        return column if isinstance(column, float) else column[rows_i, :]

    def ice_row(rows_i):
        s = rows_i.start // (cells // 2) * 2
        return jnp.where(lane_of < cells // 2, ice(s), ice(s + 1))

    def first_sweep():
        def field(r, rows_i):
            return vel_ref[r, rows_i, :].astype(jnp.float32)

        up_x, up_y, visc_x, visc_y, sxx_x, sxy_x, sxy_y, syy_y = outside(0, field(0, slice(0, 1)), field(1, slice(0, 1)))
        *columns, visc_y = as_columns(up_y[0], up_y[1], sxy_y, syy_y, visc_y)

        def apply(rows_i, start, push):
            visc, fric = visc_ref[rows_i, :], fric_ref[rows_i, :]
            before = visc_x if rows_i.start == 0 else visc_ref[rows_i.start - 1 : rows_i.start, :]
            behind_x, behind_y = lower_x(visc, before), lower_y(visc, visc_y[rows_i, :])
            diag = (5.0 * visc + 4.0 * behind_x + behind_y, 5.0 * visc + behind_x + 4.0 * behind_y)
            for r in range(2):
                relax_r = 1.0 / (diag[r] + fric)
                relax[r, rows_i, :] = OMEGA * relax_r
                moved = relax_r * (drive_ref[r, rows_i, :].astype(jnp.float32) - push[r] - fric * start[r])
                gain[r, rows_i, :] = ice_row(rows_i) * (OMEGA * relax_r) * (moved + start[r])
                first[r, rows_i, :] = start[r] + OMEGA * moved

        stress_images(field, up_x, columns[:2], sxx_x, sxy_x, columns[2], columns[3], apply)
        send_edges(1, first.at[0], first.at[1])

    def second_sweep():
        def field(r, rows_i):
            return first[r, rows_i, :]

        up_x, up_y, _, _, sxx_x, sxy_x, sxy_y, syy_y = outside(1, field(0, slice(0, 1)), field(1, slice(0, 1)))
        columns = as_columns(up_y[0], up_y[1], sxy_y, syy_y)

        def apply(rows_i, start, push):
            fric = fric_ref[rows_i, :]
            for r in range(2):
                residual = drive_ref[r, rows_i, :].astype(jnp.float32) - push[r] - fric * start[r]
                moved = relax[r, rows_i, :] * residual
                q_two[r, rows_i, :] = ice_row(rows_i) * ((1.0 / OMEGA) * moved + start[r])
                second[r, rows_i, :] = start[r] + moved

        stress_images(field, up_x, columns[:2], sxx_x, sxy_x, columns[2], columns[3], apply)
        gains = columns_of((False, gain.at[0]), (False, gain.at[1]), (True, gain.at[0]), (True, gain.at[1]))
        gain_edge[0:4, :] = gains[0:4]

    def adjoint():
        def field(r, rows_i):
            return lift[r, rows_i, :]

        send_edges(2, lift.at[0], lift.at[1])

        def apply(rows_i, lifted, push):
            fric = fric_ref[rows_i, :]
            total = None
            for r in range(2):
                back = push[r] - misfit[r, rows_i, :] + fric * lifted[r]
                term = gain[r, rows_i, :] * back - q_two[r, rows_i, :] * lifted[r]
                total = term if total is None else total + term
            out_ref[rows_i, :] = total

        zero = jnp.zeros((1, cells), jnp.float32)
        stress_images(field, (zero, zero), (0.0, 0.0), zero, zero, 0.0, 0.0, apply)
        wait_sends()
        up_x, up_y, _, _, sxx_x, sxy_x, sxy_y, syy_y = outside(2, field(0, slice(0, 1)), field(1, slice(0, 1)))
        end = slice(cells - 1, cells)
        visc = visc_ref[end, :]
        sxx, syy, sxy = 4.0 * visc * up_x[0], 2.0 * visc * up_x[0], visc * up_x[1]
        push_u = lower_y(sxy, 0.0) - sxy - sxx
        push_v = lower_y(syy, 0.0) - syy - sxy
        out_ref[0:1, :] += gain[0, 0:1, :] * sxx_x + gain[1, 0:1, :] * sxy_x
        out_ref[end, :] += gain[0, end, :] * push_u + gain[1, end, :] * push_v
        visc = edge[0, 3, 2:3, :]
        sxx, syy, sxy = 2.0 * visc * up_y[1], 4.0 * visc * up_y[1], visc * up_y[0]
        push_u = lower_y(sxx, 0.0) - sxx - sxy
        push_v = lower_y(sxy, 0.0) - sxy - syy
        column_first, column_last = as_columns(
            gain_edge[0:1, :] * sxy_y + gain_edge[1:2, :] * syy_y,
            gain_edge[2:3, :] * push_u + gain_edge[3:4, :] * push_v,
        )
        lane = lane_of[:, :128]
        out_ref[:, :128] += jnp.where(lane == 0, column_first, 0.0)
        out_ref[:, cells - 128 :] += jnp.where(lane == 127, column_last, 0.0)

    def ice(s):
        return ice_ref[s // 2, s % 2].astype(jnp.float32)

    width = scenes * ROWS
    diagonal = lax.broadcasted_iota(jnp.int32, (ROWS, width), 0) == lax.bitwise_and(
        lax.broadcasted_iota(jnp.int32, (ROWS, width), 1), ROWS - 1
    )

    def fill(source, block):
        key, weight = block[0:1, :], block[1:2, :]
        for distance in range(NZ):
            owner = lax.rem(z + distance, NZ) * NX + x
            for slot in range(SLOTS):
                want = (owner * SLOTS + slot).astype(jnp.float32)
                chosen = jnp.where(key == want, weight, 0.0)
                at = (distance * SLOTS + slot) * ROWS
                table[at : at + ROWS, source * width : (source + 1) * width] = jnp.where(
                    diagonal, chosen, 0.0
                ).astype(jnp.bfloat16)

    for load in loads[3:]:
        load.wait()
    send_edges(0, vel_ref[0].astype(jnp.float32), vel_ref[1].astype(jnp.float32), visc_ref)
    fill(0, meta_ref[...])
    for peer in range(3):
        meta_send(peer).wait_recv()
        fill(1 + peer, meta[peer])
    ones = jnp.ones((4 * width, 128), jnp.bfloat16)
    total_w = jnp.dot(table[...], ones, preferred_element_type=jnp.float32)
    part_w[...] = jnp.zeros_like(part_w)
    for distance in range(NZ):
        for slot in range(SLOTS):
            at = (distance * SLOTS + slot) * ROWS
            place = NZ if distance == NZ // 2 and slot >= 2 else distance
            part_w[place, slot : slot + 1, :] = total_w[at : at + 1, :]
    ring_send_w(0, 1).start()
    ring_send_w(1, 1).start()
    for c in range(chunks):
        own_load(c).wait()
    def at_chunk(c, action):
        pl.when(jnp.logical_and(c >= 0, c < chunks))(lambda: action(c))

    def combine(c):
        for side in range(2):
            far_send(side, c).wait_recv()
        columns = []
        for h in range(ROWS // 16):
            columns.append(
                jnp.concatenate(
                    [ag[s, c, :, h * 16 : (h + 1) * 16, :].reshape(scenes * 16, 128) for s in range(4)], axis=0
                )
            )
        stacked = columns[0] if len(columns) == 1 else jnp.concatenate(columns, axis=1)
        sums = jnp.dot(table[...], stacked, preferred_element_type=jnp.float32)
        part[c] = sums.reshape(NZ, SLOTS, ROWS, 128)
        ring_send(0, 1, c).start()
        ring_send(1, 1, c).start()

    def ring_step(stage, c):
        for side in range(2):
            ring_send(side, stage - 1, c).wait_recv()
            mine = 5 - stage if side == 0 else 3 + stage
            if stage == 2:
                part[c, mine, side * 2 : side * 2 + 2] += (rp1, rm1)[side][c]
            else:
                part[c, mine] += (rp, rm)[side][stage - 3, c]
            ring_send(side, stage, c).start()

    def finish(c):
        for side in range(2):
            ring_send(side, 4, c).wait_recv()
        obs_sum = part[c, 0] + (rp[2, c] + rm[2, c])
        tile = cells // 2
        component = c // (chunks // 2)
        offset = lax.rem(c, chunks // 2) * ROWS
        for s in range(SLOTS):
            at = (
                component,
                pl.ds(pl.multiple_of(s // 2 * tile + offset, ROWS), ROWS),
                slice(s % 2 * tile, s % 2 * tile + tile),
            )
            value = ice(s) * (part_w[0, s : s + 1, :] * second[at] - obs_sum[s])
            misfit[at] = value
            lift[at] = relax[at] * value

    def ring_step_w(stage):
        for side in range(2):
            ring_send_w(side, stage - 1).wait_recv()
            mine = 5 - stage if side == 0 else 3 + stage
            part_w[mine] += rw[side * 4 + stage - 2]
            ring_send_w(side, stage).start()

    def finish_w():
        for side in range(2):
            ring_send_w(side, 4).wait_recv()
        part_w[0] += rw[3] + rw[7]

    def wait_sends():
        def drain(c, carry):
            for side in range(2):
                own_send(side, c).wait_send()
                far_send(side, c).wait_send()
                for stage in range(1, 5):
                    ring_send(side, stage, c).wait_send()
            return carry

        lax.fori_loop(0, chunks, drain, 0)
        for peer in range(3):
            meta_send(peer).wait_send()
        for side in range(2):
            for stage in range(1, 5):
                ring_send_w(side, stage).wait_send()

    def step(k, carry):
        @pl.when(k < chunks)
        def _():
            for side in range(2):
                own_send(side, k).wait_recv()
                far_send(side, k).start()

        @pl.when(k + LEAD < chunks)
        def _():
            own_send(0, k + LEAD).start()
            own_send(1, k + LEAD).start()

        pl.when(k == 1 + 4 * GAP)(finish_w)
        at_chunk(k - 1 - 4 * GAP, finish)
        for stage in (4, 3, 2):
            at_chunk(k - 1 - (stage - 1) * GAP, functools.partial(ring_step, stage))
            pl.when(k == 2 * stage - 3)(functools.partial(ring_step_w, stage))
        at_chunk(k - 1, combine)
        pl.when(k == 0)(first_sweep)
        pl.when(k == 2)(second_sweep)
        return carry

    lax.fori_loop(0, chunks + 1 + 4 * GAP, step, 0)
    adjoint()
    for e in range(3):
        for place in range(6):
            edge_send(e, place).wait_send()


def body(vel0, visc, fric, drive, scene_obs, scene_weight, scene_owner, scene_slot, ice_mask):
    obs = scene_obs[0]
    cells = visc.shape[0]
    scenes, _, tile, _ = obs.shape
    height = 2 * tile
    chunks = height // ROWS
    f32, bf16 = jnp.float32, jnp.bfloat16
    dma = pltpu.SemaphoreType.DMA
    return pl.pallas_call(
        exchange_kernel,
        out_shape=jax.ShapeDtypeStruct((cells, cells), f32),
        in_specs=[
            pl.BlockSpec(memory_space=pltpu.HBM)
        ] * 9,
        out_specs=pl.BlockSpec(memory_space=pltpu.VMEM),
        scratch_shapes=[
            pltpu.VMEM((1, scenes), jnp.int32),
            pltpu.VMEM((1, scenes), jnp.int32),
            pltpu.VMEM((1, scenes), bf16),
            pltpu.SMEM((2, 2), jnp.int32),
            pltpu.VMEM((2, cells, cells), bf16),
            pltpu.VMEM((cells, cells), f32),
            pltpu.VMEM((cells, cells), f32),
            pltpu.VMEM((2, cells, cells), bf16),
            pltpu.VMEM((8, scenes * ROWS), f32),
            *[pltpu.VMEM((2, cells, cells), f32)] * 7,
            pltpu.VMEM((3, 4, 8, cells), f32),
            pltpu.VMEM((3, 6, 8, cells), f32),
            pltpu.VMEM((8, cells), f32),
            pltpu.VMEM((3, 8, scenes * ROWS), f32),
            pltpu.VMEM((4, chunks, scenes, ROWS, tile), bf16),
            pltpu.VMEM((NZ * SLOTS * ROWS, 4 * scenes * ROWS), bf16),
            pltpu.VMEM((chunks, NZ, SLOTS, ROWS, tile), f32),
            pltpu.VMEM((NZ + 1, 8, 128), f32),
            pltpu.VMEM((chunks, 2, ROWS, tile), f32),
            pltpu.VMEM((3, chunks, SLOTS, ROWS, tile), f32),
            pltpu.VMEM((chunks, 2, ROWS, tile), f32),
            pltpu.VMEM((3, chunks, SLOTS, ROWS, tile), f32),
            pltpu.VMEM((8, 8, 128), f32),
            dma((chunks,)),
            dma((3,)), dma((3,)),
            dma((4, chunks)), dma((4, chunks)),
            dma((8, chunks)), dma((8, chunks)),
            dma((8,)), dma((8,)),
            dma((3, 6)), dma((3, 6)),
            dma((8,)),
        ],
        compiler_params=pltpu.CompilerParams(
            collective_id=0, has_side_effects=True, vmem_limit_bytes=67043328
        ),
    )(scene_owner.reshape(1, scenes), scene_slot, scene_weight, ice_mask, vel0, visc, fric, drive, obs.reshape(scenes, height, tile))


def solution(mesh):
    placed = (
        P(None, "gx", "gy"),
        P("gx", "gy"),
        P("gx", "gy"),
        P(None, "gx", "gy"),
        P("gy", "gx", None, None, None),
        P("gy", "gx"),
        P("gy", "gx", None),
        P("gy", "gx"),
        P("gx", "gy"),
    )
    return jax.shard_map(body, mesh=mesh, in_specs=placed, out_specs=P("gx", "gy"), check_vma=False)
```

```python
import functools

import jax
import jax.numpy as jnp
from jax import lax
from jax.experimental import pallas as pl
from jax.experimental.pallas import tpu as pltpu
from jax.sharding import PartitionSpec as P

OMEGA = 0.6
NX, NZ = 4, 8
SLOTS = 4
STRIP = 32
ROWS = 16
LEAD = 3
GAP = 2
MESH = pl.DeviceIdType.MESH


def exchange_kernel(
    owner_in, slot_in, weight_in, ice_in, vel_in, visc_in, fric_in, drive_in, obs_ref, out_ref,
    owner_ref, slot_ref, weight_ref, ice_ref, vel_ref, visc_ref, fric_ref, drive_ref, meta_ref,
    relax, first, second, gain, q_two, misfit, lift, edge, halo, gain_edge,
    meta, ag, table, part, part_w, rp1, rp, rm1, rm, rw,
    own_sem, meta_s, meta_r, ag_s, ag_r, rs_s, rs_r, rw_s, rw_r, edge_s, edge_r, load_sem,
):
    chunks = ag.shape[1]
    scenes = ag.shape[2]
    half = scenes // 2
    me_x, me_y = lax.axis_index("gx"), lax.axis_index("gy")
    x, z = lax.rem(me_x, NX), me_x // NX
    x_right = (z * NX + lax.rem(x + 1, NX), me_y)
    x_left = (z * NX + lax.rem(x + NX - 1, NX), me_y)
    x_far = (z * NX + lax.rem(x + 2, NX), me_y)
    z_right = (lax.rem(z + 1, NZ) * NX + x, me_y)
    z_left = (lax.rem(z + NZ - 1, NZ) * NX + x, me_y)

    gx_next, gx_back = lax.rem(me_x + 1, NX * NZ), lax.rem(me_x + NX * NZ - 1, NX * NZ)
    side_y = lax.axis_size("gy")
    gy_next, gy_back = lax.rem(me_y + 1, side_y), lax.rem(me_y + side_y - 1, side_y)
    at_first_x, at_last_x = me_x == 0, me_x == NX * NZ - 1
    at_first_y, at_last_y = me_y == 0, me_y == side_y - 1
    edges = (
        (0, (gx_back, me_y)),
        (1, (gx_next, me_y)),
        (2, (me_x, gy_back)),
        (3, (me_x, gy_next)),
        (1, (gx_next, gy_back)),
        (0, (gx_back, gy_next)),
    )

    def remote(src, dst, send, recv, device):
        return pltpu.make_async_remote_copy(
            src_ref=src, dst_ref=dst, send_sem=send, recv_sem=recv, device_id=device, device_id_type=MESH
        )

    def component_of(c):
        return lax.rem(c, 2)

    def offset_of(c):
        return lax.rem((c // 2) * (chunks // 2 - 1), chunks // 2) * ROWS

    def rows(c):
        start = component_of(c) * (chunks // 2 * ROWS) + offset_of(c)
        return pl.ds(pl.multiple_of(start, ROWS), ROWS)

    def own_load(c):
        return pltpu.make_async_copy(obs_ref.at[:, rows(c), :], ag.at[0, c], own_sem.at[c])

    def own_send(side, c):
        return remote(
            obs_ref.at[:, rows(c), :], ag.at[1 + side, c], ag_s.at[side, c], ag_r.at[side, c],
            (x_right, x_left)[side],
        )

    def far_send(side, c):
        piece = pl.ds(side * half, half)
        return remote(
            ag.at[1 + side, c, piece], ag.at[3, c, piece], ag_s.at[2 + side, c], ag_r.at[2 + side, c],
            (x_right, x_left)[side],
        )

    def meta_send(peer):
        return remote(
            meta_ref, meta.at[peer], meta_s.at[peer], meta_r.at[peer], (x_right, x_left, x_far)[peer]
        )

    def ring_send(side, stage, c):
        device = (z_right, z_left)[side]
        semaphores = (rs_s.at[side * 4 + stage - 1, c], rs_r.at[side * 4 + stage - 1, c])
        if stage == 1:
            return remote(
                part.at[c, 4, pl.ds(side * 2, 2)], (rp1, rm1)[side].at[c], *semaphores, device
            )
        source = 5 - stage if side == 0 else 3 + stage
        return remote(part.at[c, source], (rp, rm)[side].at[stage - 2, c], *semaphores, device)

    def ring_send_w(side, stage):
        source = 5 - stage if side == 0 else (8 if stage == 1 else 3 + stage)
        index = side * 4 + stage - 1
        return remote(
            part_w.at[source], rw.at[index], rw_s.at[index], rw_r.at[index], (z_right, z_left)[side]
        )

    def edge_send(e, place):
        message, device = edges[place]
        return remote(
            edge.at[e, message], halo.at[e, place], edge_s.at[e, place], edge_r.at[e, place], device
        )

    barrier = pltpu.get_barrier_semaphore()
    for device in (x_right, x_left, x_far, z_right, z_left, *(device for _, device in edges)):
        pl.semaphore_signal(barrier, inc=1, device_id=device, device_id_type=MESH)
    pairs = (
        (owner_in, owner_ref), (slot_in, slot_ref), (weight_in, weight_ref), (vel_in, vel_ref),
        (visc_in, visc_ref), (fric_in, fric_ref), (drive_in, drive_ref), (ice_in, ice_ref),
    )
    loads = [pltpu.make_async_copy(a, b, load_sem.at[n]) for n, (a, b) in enumerate(pairs)]
    for load in loads:
        load.start()
    for c in range(chunks):
        own_load(c).start()
    for load in loads[:3]:
        load.wait()
    key = (owner_ref[...] * SLOTS + slot_ref[...]).astype(jnp.float32)
    place = lax.broadcasted_iota(jnp.int32, (scenes, scenes), 0)
    same = place == lax.broadcasted_iota(jnp.int32, (scenes, scenes), 1)
    spread = lax.broadcasted_iota(jnp.int32, (scenes, scenes * ROWS), 1) // ROWS
    spread = spread == lax.broadcasted_iota(jnp.int32, (scenes, scenes * ROWS), 0)
    for r, value in enumerate((key, weight_ref[...].astype(jnp.float32))):
        column = jnp.sum(jnp.where(same, value, 0.0), axis=1, keepdims=True)
        meta_ref[r : r + 1, :] = jnp.sum(jnp.where(spread, column, 0.0), axis=0, keepdims=True)
    pl.semaphore_wait(barrier, 11)

    for peer in range(3):
        meta_send(peer).start()
    for c in range(LEAD):
        own_send(0, c).start()
        own_send(1, c).start()

    cells = visc_ref.shape[0]
    lane_of = lax.broadcasted_iota(jnp.int32, (1, cells), 1)

    def columns_of(*columns):
        lane, packed = lane_of[:, :128], None
        for n, (last, array) in enumerate(columns):
            block = array[:, cells - 128 :] if last else array[:, :128]
            moved = (n + 1 if last else n) % 128
            block = pltpu.roll(block, moved, 1) if moved else block
            packed = block if packed is None else jnp.where(lane == n, block, packed)
        return packed.T

    def send_rows(e, u, v, visc=None):
        for r, array in enumerate((u, v)):
            edge[e, 0, r : r + 1, :] = array[0:1, :]
            edge[e, 1, r : r + 1, :] = array[cells - 1 :, :]
        if visc is not None:
            edge[e, 1, 2:3, :] = visc[cells - 1 :, :]
        for place in (0, 1, 4, 5):
            edge_send(e, place).start()

    def send_columns(e, u, v, visc=None):
        columns = [(False, u), (False, v), (True, u), (True, v)]
        if visc is not None:
            columns.append((True, visc))
        turned = columns_of(*columns)
        edge[e, 2, 0:2, :] = turned[0:2]
        edge[e, 3, 0:3, :] = turned[2:5]
        for place in (2, 3):
            edge_send(e, place).start()

    def send_edges(*field):
        send_rows(*field)
        send_columns(*field)

    def outside(e, u_first, v_first):
        for place in range(6):
            edge_send(e, place).wait_recv()

        def got(place, r):
            return halo[e, place, r : r + 1, :]

        zero = jnp.zeros((1, cells), jnp.float32)
        up_x = [jnp.where(at_last_x, zero, got(0, r)) for r in range(2)]
        up_y = [jnp.where(at_last_y, zero, got(2, r)) for r in range(2)]
        visc_x = jnp.where(at_first_x, zero, halo[0, 1, 2:3, :])
        visc_y = jnp.where(at_first_y, zero, halo[0, 3, 2:3, :])
        back_x = [got(1, r) for r in range(2)]
        back_y = [got(3, r) for r in range(2)]
        back_x_up, back_y_up = [], []
        for r in range(2):
            corner = jnp.where(at_last_y, 0.0, halo[e, 4, r : r + 1, 0:1])
            back_x_up.append(jnp.where(lane_of == cells - 1, corner, pltpu.roll(back_x[r], cells - 1, 1)))
            corner = jnp.where(at_last_x, 0.0, halo[e, 5, r : r + 1, cells - 1 : cells])
            back_y_up.append(jnp.where(lane_of == cells - 1, corner, pltpu.roll(back_y[r], cells - 1, 1)))
        sxx_x = visc_x * (4.0 * (u_first - back_x[0]) + 2.0 * (back_x_up[1] - back_x[1]))
        sxy_x = visc_x * ((back_x_up[0] - back_x[0]) + (v_first - back_x[1]))
        u_y, v_y = edge[e, 2, 0:1, :], edge[e, 2, 1:2, :]
        sxy_y = visc_y * ((u_y - back_y[0]) + (back_y_up[1] - back_y[1]))
        syy_y = visc_y * (4.0 * (v_y - back_y[1]) + 2.0 * (back_y_up[0] - back_y[0]))
        return up_x, up_y, visc_x, visc_y, sxx_x, sxy_x, sxy_y, syy_y

    def as_columns(*rows):
        zero = jnp.zeros((8 - len(rows), cells), jnp.float32)
        turned = jnp.concatenate([*rows, zero], axis=0).T
        return [turned[:, n : n + 1] for n in range(len(rows))]

    strip_row = lax.broadcasted_iota(jnp.int32, (STRIP, 1), 0)

    def upper_x(field, row):
        return jnp.where(strip_row == STRIP - 1, row, pltpu.roll(field, STRIP - 1, 0))

    def lower_x(field, row):
        return jnp.where(strip_row == 0, row, pltpu.roll(field, 1, 0))

    def upper_y(field, column):
        return jnp.where(lane_of == cells - 1, column, pltpu.roll(field, cells - 1, 1))

    def lower_y(field, column):
        return jnp.where(lane_of == 0, column, pltpu.roll(field, 1, 1))

    def stress_images(field, up_x, up_y, sxx_x, sxy_x, sxy_y, syy_y, apply):
        for i in range(0, cells, STRIP):
            rows_i = slice(i, i + STRIP)
            u, v = field(0, rows_i), field(1, rows_i)
            following = slice(i + STRIP, i + STRIP + 1)
            after = up_x if i + STRIP == cells else [field(r, following) for r in range(2)]
            a_x, b_x = upper_x(u, after[0]) - u, upper_x(v, after[1]) - v
            a_y = upper_y(u, take(up_y[0], rows_i)) - u
            b_y = upper_y(v, take(up_y[1], rows_i)) - v
            visc = visc_ref[rows_i, :]
            sxx = visc * (4.0 * a_x + 2.0 * b_y)
            syy = visc * (4.0 * b_y + 2.0 * a_x)
            sxy = visc * (a_y + b_x)
            push_u = lower_x(sxx, sxx_x) - sxx + lower_y(sxy, take(sxy_y, rows_i)) - sxy
            push_v = lower_x(sxy, sxy_x) - sxy + lower_y(syy, take(syy_y, rows_i)) - syy
            apply(rows_i, (u, v), (push_u, push_v))
            sxx_x, sxy_x = sxx[STRIP - 1 :, :], sxy[STRIP - 1 :, :]

    def take(column, rows_i):
        return column if isinstance(column, float) else column[rows_i, :]

    def ice_row(rows_i):
        s = rows_i.start // (cells // 2) * 2
        return jnp.where(lane_of < cells // 2, ice(s), ice(s + 1))

    def first_sweep():
        def field(r, rows_i):
            return vel_ref[r, rows_i, :].astype(jnp.float32)

        up_x, up_y, visc_x, visc_y, sxx_x, sxy_x, sxy_y, syy_y = outside(0, field(0, slice(0, 1)), field(1, slice(0, 1)))
        *columns, visc_y = as_columns(up_y[0], up_y[1], sxy_y, syy_y, visc_y)

        def apply(rows_i, start, push):
            visc, fric = visc_ref[rows_i, :], fric_ref[rows_i, :]
            before = visc_x if rows_i.start == 0 else visc_ref[rows_i.start - 1 : rows_i.start, :]
            behind_x, behind_y = lower_x(visc, before), lower_y(visc, visc_y[rows_i, :])
            diag = (5.0 * visc + 4.0 * behind_x + behind_y, 5.0 * visc + behind_x + 4.0 * behind_y)
            for r in range(2):
                relax_r = 1.0 / (diag[r] + fric)
                relax[r, rows_i, :] = OMEGA * relax_r
                moved = relax_r * (drive_ref[r, rows_i, :].astype(jnp.float32) - push[r] - fric * start[r])
                gain[r, rows_i, :] = ice_row(rows_i) * (OMEGA * relax_r) * (moved + start[r])
                first[r, rows_i, :] = start[r] + OMEGA * moved

        stress_images(field, up_x, columns[:2], sxx_x, sxy_x, columns[2], columns[3], apply)
        send_edges(1, first.at[0], first.at[1])

    def second_sweep():
        def field(r, rows_i):
            return first[r, rows_i, :]

        up_x, up_y, _, _, sxx_x, sxy_x, sxy_y, syy_y = outside(1, field(0, slice(0, 1)), field(1, slice(0, 1)))
        columns = as_columns(up_y[0], up_y[1], sxy_y, syy_y)

        def apply(rows_i, start, push):
            fric = fric_ref[rows_i, :]
            for r in range(2):
                residual = drive_ref[r, rows_i, :].astype(jnp.float32) - push[r] - fric * start[r]
                moved = relax[r, rows_i, :] * residual
                q_two[r, rows_i, :] = ice_row(rows_i) * ((1.0 / OMEGA) * moved + start[r])
                second[r, rows_i, :] = start[r] + moved

        stress_images(field, up_x, columns[:2], sxx_x, sxy_x, columns[2], columns[3], apply)
        gains = columns_of((False, gain.at[0]), (False, gain.at[1]), (True, gain.at[0]), (True, gain.at[1]))
        gain_edge[0:4, :] = gains[0:4]

    def adjoint():
        def field(r, rows_i):
            return lift[r, rows_i, :]

        send_columns(2, lift.at[0], lift.at[1])

        def apply(rows_i, lifted, push):
            fric = fric_ref[rows_i, :]
            total = None
            for r in range(2):
                back = push[r] - misfit[r, rows_i, :] + fric * lifted[r]
                term = gain[r, rows_i, :] * back - q_two[r, rows_i, :] * lifted[r]
                total = term if total is None else total + term
            out_ref[rows_i, :] = total

        zero = jnp.zeros((1, cells), jnp.float32)
        stress_images(field, (zero, zero), (0.0, 0.0), zero, zero, 0.0, 0.0, apply)
        wait_sends()
        up_x, up_y, _, _, sxx_x, sxy_x, sxy_y, syy_y = outside(2, field(0, slice(0, 1)), field(1, slice(0, 1)))
        end = slice(cells - 1, cells)
        visc = visc_ref[end, :]
        sxx, syy, sxy = 4.0 * visc * up_x[0], 2.0 * visc * up_x[0], visc * up_x[1]
        push_u = lower_y(sxy, 0.0) - sxy - sxx
        push_v = lower_y(syy, 0.0) - syy - sxy
        out_ref[0:1, :] += gain[0, 0:1, :] * sxx_x + gain[1, 0:1, :] * sxy_x
        out_ref[end, :] += gain[0, end, :] * push_u + gain[1, end, :] * push_v
        visc = edge[0, 3, 2:3, :]
        sxx, syy, sxy = 2.0 * visc * up_y[1], 4.0 * visc * up_y[1], visc * up_y[0]
        push_u = lower_y(sxx, 0.0) - sxx - sxy
        push_v = lower_y(sxy, 0.0) - sxy - syy
        column_first, column_last = as_columns(
            gain_edge[0:1, :] * sxy_y + gain_edge[1:2, :] * syy_y,
            gain_edge[2:3, :] * push_u + gain_edge[3:4, :] * push_v,
        )
        lane = lane_of[:, :128]
        out_ref[:, :128] += jnp.where(lane == 0, column_first, 0.0)
        out_ref[:, cells - 128 :] += jnp.where(lane == 127, column_last, 0.0)

    def ice(s):
        return ice_ref[s // 2, s % 2].astype(jnp.float32)

    width = scenes * ROWS
    diagonal = lax.broadcasted_iota(jnp.int32, (ROWS, width), 0) == lax.bitwise_and(
        lax.broadcasted_iota(jnp.int32, (ROWS, width), 1), ROWS - 1
    )

    def fill(source, block):
        key, weight = block[0:1, :], block[1:2, :]
        for distance in range(NZ):
            owner = lax.rem(z + distance, NZ) * NX + x
            for slot in range(SLOTS):
                want = (owner * SLOTS + slot).astype(jnp.float32)
                chosen = jnp.where(key == want, weight, 0.0)
                at = (distance * SLOTS + slot) * ROWS
                table[at : at + ROWS, source * width : (source + 1) * width] = jnp.where(
                    diagonal, chosen, 0.0
                ).astype(jnp.bfloat16)

    for load in loads[3:]:
        load.wait()
    send_edges(0, vel_ref[0].astype(jnp.float32), vel_ref[1].astype(jnp.float32), visc_ref)
    fill(0, meta_ref[...])
    for peer in range(3):
        meta_send(peer).wait_recv()
        fill(1 + peer, meta[peer])
    ones = jnp.ones((4 * width, 128), jnp.bfloat16)
    total_w = jnp.dot(table[...], ones, preferred_element_type=jnp.float32)
    part_w[...] = jnp.zeros_like(part_w)
    for distance in range(NZ):
        for slot in range(SLOTS):
            at = (distance * SLOTS + slot) * ROWS
            place = NZ if distance == NZ // 2 and slot >= 2 else distance
            part_w[place, slot : slot + 1, :] = total_w[at : at + 1, :]
    ring_send_w(0, 1).start()
    ring_send_w(1, 1).start()
    for c in range(chunks):
        own_load(c).wait()
    def at_chunk(c, action):
        pl.when(jnp.logical_and(c >= 0, c < chunks))(lambda: action(c))

    def combine(c):
        for side in range(2):
            far_send(side, c).wait_recv()
        columns = []
        for h in range(ROWS // 16):
            columns.append(
                jnp.concatenate(
                    [ag[s, c, :, h * 16 : (h + 1) * 16, :].reshape(scenes * 16, 128) for s in range(4)], axis=0
                )
            )
        stacked = columns[0] if len(columns) == 1 else jnp.concatenate(columns, axis=1)
        sums = jnp.dot(table[...], stacked, preferred_element_type=jnp.float32)
        part[c] = sums.reshape(NZ, SLOTS, ROWS, 128)
        ring_send(0, 1, c).start()
        ring_send(1, 1, c).start()

    def ring_step(stage, c):
        for side in range(2):
            ring_send(side, stage - 1, c).wait_recv()
            mine = 5 - stage if side == 0 else 3 + stage
            if stage == 2:
                part[c, mine, side * 2 : side * 2 + 2] += (rp1, rm1)[side][c]
            else:
                part[c, mine] += (rp, rm)[side][stage - 3, c]
            ring_send(side, stage, c).start()

    def finish(c):
        for side in range(2):
            ring_send(side, 4, c).wait_recv()
        obs_sum = part[c, 0] + (rp[2, c] + rm[2, c])
        tile = cells // 2
        component, offset = component_of(c), offset_of(c)
        for s in range(SLOTS):
            at = (
                component,
                pl.ds(pl.multiple_of(s // 2 * tile + offset, ROWS), ROWS),
                slice(s % 2 * tile, s % 2 * tile + tile),
            )
            value = ice(s) * (part_w[0, s : s + 1, :] * second[at] - obs_sum[s])
            misfit[at] = value
            lift[at] = relax[at] * value

    def ring_step_w(stage):
        for side in range(2):
            ring_send_w(side, stage - 1).wait_recv()
            mine = 5 - stage if side == 0 else 3 + stage
            part_w[mine] += rw[side * 4 + stage - 2]
            ring_send_w(side, stage).start()

    def finish_w():
        for side in range(2):
            ring_send_w(side, 4).wait_recv()
        part_w[0] += rw[3] + rw[7]

    def wait_sends():
        def drain(c, carry):
            for side in range(2):
                own_send(side, c).wait_send()
                far_send(side, c).wait_send()
                for stage in range(1, 5):
                    ring_send(side, stage, c).wait_send()
            return carry

        lax.fori_loop(0, chunks, drain, 0)
        for peer in range(3):
            meta_send(peer).wait_send()
        for side in range(2):
            for stage in range(1, 5):
                ring_send_w(side, stage).wait_send()

    def step(k, carry):
        @pl.when(k < chunks)
        def _():
            for side in range(2):
                own_send(side, k).wait_recv()
                far_send(side, k).start()

        @pl.when(k + LEAD < chunks)
        def _():
            own_send(0, k + LEAD).start()
            own_send(1, k + LEAD).start()

        pl.when(k == 1 + 4 * GAP)(finish_w)
        at_chunk(k - 1 - 4 * GAP, finish)
        pl.when(k == 4 + 4 * GAP)(lambda: send_rows(2, lift.at[0], lift.at[1]))
        for stage in (4, 3, 2):
            at_chunk(k - 1 - (stage - 1) * GAP, functools.partial(ring_step, stage))
            pl.when(k == 2 * stage - 3)(functools.partial(ring_step_w, stage))
        at_chunk(k - 1, combine)
        pl.when(k == 0)(first_sweep)
        pl.when(k == 2)(second_sweep)
        return carry

    lax.fori_loop(0, chunks + 1 + 4 * GAP, step, 0)
    adjoint()
    for e in range(3):
        for place in range(6):
            edge_send(e, place).wait_send()


def body(vel0, visc, fric, drive, scene_obs, scene_weight, scene_owner, scene_slot, ice_mask):
    obs = scene_obs[0]
    cells = visc.shape[0]
    scenes, _, tile, _ = obs.shape
    height = 2 * tile
    chunks = height // ROWS
    f32, bf16 = jnp.float32, jnp.bfloat16
    dma = pltpu.SemaphoreType.DMA
    return pl.pallas_call(
        exchange_kernel,
        out_shape=jax.ShapeDtypeStruct((cells, cells), f32),
        in_specs=[
            pl.BlockSpec(memory_space=pltpu.HBM)
        ] * 9,
        out_specs=pl.BlockSpec(memory_space=pltpu.VMEM),
        scratch_shapes=[
            pltpu.VMEM((1, scenes), jnp.int32),
            pltpu.VMEM((1, scenes), jnp.int32),
            pltpu.VMEM((1, scenes), bf16),
            pltpu.SMEM((2, 2), jnp.int32),
            pltpu.VMEM((2, cells, cells), bf16),
            pltpu.VMEM((cells, cells), f32),
            pltpu.VMEM((cells, cells), f32),
            pltpu.VMEM((2, cells, cells), bf16),
            pltpu.VMEM((8, scenes * ROWS), f32),
            *[pltpu.VMEM((2, cells, cells), f32)] * 7,
            pltpu.VMEM((3, 4, 8, cells), f32),
            pltpu.VMEM((3, 6, 8, cells), f32),
            pltpu.VMEM((8, cells), f32),
            pltpu.VMEM((3, 8, scenes * ROWS), f32),
            pltpu.VMEM((4, chunks, scenes, ROWS, tile), bf16),
            pltpu.VMEM((NZ * SLOTS * ROWS, 4 * scenes * ROWS), bf16),
            pltpu.VMEM((chunks, NZ, SLOTS, ROWS, tile), f32),
            pltpu.VMEM((NZ + 1, 8, 128), f32),
            pltpu.VMEM((chunks, 2, ROWS, tile), f32),
            pltpu.VMEM((3, chunks, SLOTS, ROWS, tile), f32),
            pltpu.VMEM((chunks, 2, ROWS, tile), f32),
            pltpu.VMEM((3, chunks, SLOTS, ROWS, tile), f32),
            pltpu.VMEM((8, 8, 128), f32),
            dma((chunks,)),
            dma((3,)), dma((3,)),
            dma((4, chunks)), dma((4, chunks)),
            dma((8, chunks)), dma((8, chunks)),
            dma((8,)), dma((8,)),
            dma((3, 6)), dma((3, 6)),
            dma((8,)),
        ],
        compiler_params=pltpu.CompilerParams(
            collective_id=0, has_side_effects=True, vmem_limit_bytes=67043328
        ),
    )(scene_owner.reshape(1, scenes), scene_slot, scene_weight, ice_mask, vel0, visc, fric, drive, obs.reshape(scenes, height, tile))


def solution(mesh):
    placed = (
        P(None, "gx", "gy"),
        P("gx", "gy"),
        P("gx", "gy"),
        P(None, "gx", "gy"),
        P("gy", "gx", None, None, None),
        P("gy", "gx"),
        P("gy", "gx", None),
        P("gy", "gx"),
        P("gx", "gy"),
    )
    return jax.shard_map(body, mesh=mesh, in_specs=placed, out_specs=P("gx", "gy"), check_vma=False)
```

```python
import functools

import jax
import jax.numpy as jnp
from jax import lax
from jax.experimental import pallas as pl
from jax.experimental.pallas import tpu as pltpu
from jax.sharding import PartitionSpec as P

OMEGA = 0.6
NX, NZ = 4, 8
SLOTS = 4
STRIP = 32
ROWS = 16
LEAD = 3
GAP = 2
MESH = pl.DeviceIdType.MESH


def exchange_kernel(
    owner_in, slot_in, weight_in, ice_in, vel_in, visc_in, fric_in, drive_in, obs_ref, out_ref,
    owner_ref, slot_ref, weight_ref, ice_ref, vel_ref, visc_ref, fric_ref, drive_ref, meta_ref,
    relax, first, second, gain, q_two, misfit, lift, edge, halo, gain_edge,
    meta, ag, table, part, part_w, rp1, rp, rm1, rm, rw,
    own_sem, meta_s, meta_r, ag_s, ag_r, rs_s, rs_r, rw_s, rw_r, edge_s, edge_r, load_sem,
):
    chunks = ag.shape[1]
    scenes = ag.shape[2]
    half = scenes // 2
    me_x, me_y = lax.axis_index("gx"), lax.axis_index("gy")
    x, z = lax.rem(me_x, NX), me_x // NX
    x_right = (z * NX + lax.rem(x + 1, NX), me_y)
    x_left = (z * NX + lax.rem(x + NX - 1, NX), me_y)
    x_far = (z * NX + lax.rem(x + 2, NX), me_y)
    z_right = (lax.rem(z + 1, NZ) * NX + x, me_y)
    z_left = (lax.rem(z + NZ - 1, NZ) * NX + x, me_y)

    gx_next, gx_back = lax.rem(me_x + 1, NX * NZ), lax.rem(me_x + NX * NZ - 1, NX * NZ)
    side_y = lax.axis_size("gy")
    gy_next, gy_back = lax.rem(me_y + 1, side_y), lax.rem(me_y + side_y - 1, side_y)
    at_first_x, at_last_x = me_x == 0, me_x == NX * NZ - 1
    at_first_y, at_last_y = me_y == 0, me_y == side_y - 1
    edges = (
        (0, (gx_back, me_y)),
        (1, (gx_next, me_y)),
        (2, (me_x, gy_back)),
        (3, (me_x, gy_next)),
        (1, (gx_next, gy_back)),
        (0, (gx_back, gy_next)),
    )

    def remote(src, dst, send, recv, device):
        return pltpu.make_async_remote_copy(
            src_ref=src, dst_ref=dst, send_sem=send, recv_sem=recv, device_id=device, device_id_type=MESH
        )

    def component_of(c):
        return lax.rem(c, 2)

    def offset_of(c):
        return lax.rem((c // 2) * (chunks // 2 - 1), chunks // 2) * ROWS

    def rows(c):
        start = component_of(c) * (chunks // 2 * ROWS) + offset_of(c)
        return pl.ds(pl.multiple_of(start, ROWS), ROWS)

    def own_load(c):
        return pltpu.make_async_copy(obs_ref.at[:, rows(c), :], ag.at[0, c], own_sem.at[c])

    def own_send(side, c):
        return remote(
            obs_ref.at[:, rows(c), :], ag.at[1 + side, c], ag_s.at[side, c], ag_r.at[side, c],
            (x_right, x_left)[side],
        )

    def far_send(side, c):
        piece = pl.ds(side * half, half)
        return remote(
            ag.at[1 + side, c, piece], ag.at[3, c, piece], ag_s.at[2 + side, c], ag_r.at[2 + side, c],
            (x_right, x_left)[side],
        )

    def meta_send(peer):
        return remote(
            meta_ref, meta.at[peer], meta_s.at[peer], meta_r.at[peer], (x_right, x_left, x_far)[peer]
        )

    def ring_send(side, stage, c):
        device = (z_right, z_left)[side]
        semaphores = (rs_s.at[side * 4 + stage - 1, c], rs_r.at[side * 4 + stage - 1, c])
        if stage == 1:
            return remote(
                part.at[c, 4, pl.ds(side * 2, 2)], (rp1, rm1)[side].at[c], *semaphores, device
            )
        source = 5 - stage if side == 0 else 3 + stage
        return remote(part.at[c, source], (rp, rm)[side].at[stage - 2, c], *semaphores, device)

    def ring_send_w(side, stage):
        source = 5 - stage if side == 0 else (8 if stage == 1 else 3 + stage)
        index = side * 4 + stage - 1
        return remote(
            part_w.at[source], rw.at[index], rw_s.at[index], rw_r.at[index], (z_right, z_left)[side]
        )

    def edge_send(e, place):
        message, device = edges[place]
        return remote(
            edge.at[e, message], halo.at[e, place], edge_s.at[e, place], edge_r.at[e, place], device
        )

    barrier = pltpu.get_barrier_semaphore()
    for device in (x_right, x_left, x_far, z_right, z_left, *(device for _, device in edges)):
        pl.semaphore_signal(barrier, inc=1, device_id=device, device_id_type=MESH)
    pairs = (
        (owner_in, owner_ref), (slot_in, slot_ref), (weight_in, weight_ref), (vel_in, vel_ref),
        (visc_in, visc_ref), (fric_in, fric_ref), (drive_in, drive_ref), (ice_in, ice_ref),
    )
    loads = [pltpu.make_async_copy(a, b, load_sem.at[n]) for n, (a, b) in enumerate(pairs)]
    for load in loads:
        load.start()
    for c in range(chunks):
        own_load(c).start()
    for load in loads[:3]:
        load.wait()
    key = (owner_ref[...] * SLOTS + slot_ref[...]).astype(jnp.float32)
    place = lax.broadcasted_iota(jnp.int32, (scenes, scenes), 0)
    same = place == lax.broadcasted_iota(jnp.int32, (scenes, scenes), 1)
    spread = lax.broadcasted_iota(jnp.int32, (scenes, scenes * ROWS), 1) // ROWS
    spread = spread == lax.broadcasted_iota(jnp.int32, (scenes, scenes * ROWS), 0)
    for r, value in enumerate((key, weight_ref[...].astype(jnp.float32))):
        column = jnp.sum(jnp.where(same, value, 0.0), axis=1, keepdims=True)
        meta_ref[r : r + 1, :] = jnp.sum(jnp.where(spread, column, 0.0), axis=0, keepdims=True)
    pl.semaphore_wait(barrier, 11)

    for peer in range(3):
        meta_send(peer).start()
    for c in range(LEAD):
        own_send(0, c).start()
        own_send(1, c).start()

    cells = visc_ref.shape[0]
    lane_of = lax.broadcasted_iota(jnp.int32, (1, cells), 1)

    def columns_of(*columns):
        lane, packed = lane_of[:, :128], None
        for n, (last, array) in enumerate(columns):
            block = array[:, cells - 128 :] if last else array[:, :128]
            moved = (n + 1 if last else n) % 128
            block = pltpu.roll(block, moved, 1) if moved else block
            packed = block if packed is None else jnp.where(lane == n, block, packed)
        return packed.T

    def send_rows(e, u, v, visc=None):
        for r, array in enumerate((u, v)):
            edge[e, 0, r : r + 1, :] = array[0:1, :]
            edge[e, 1, r : r + 1, :] = array[cells - 1 :, :]
        if visc is not None:
            edge[e, 1, 2:3, :] = visc[cells - 1 :, :]
        for place in (0, 1, 4, 5):
            edge_send(e, place).start()

    def send_columns(e, u, v, visc=None):
        columns = [(False, u), (False, v), (True, u), (True, v)]
        if visc is not None:
            columns.append((True, visc))
        turned = columns_of(*columns)
        edge[e, 2, 0:2, :] = turned[0:2]
        edge[e, 3, 0:3, :] = turned[2:5]
        for place in (2, 3):
            edge_send(e, place).start()

    def send_edges(*field):
        send_rows(*field)
        send_columns(*field)

    def outside(e, u_first, v_first):
        for place in range(6):
            edge_send(e, place).wait_recv()

        def got(place, r):
            return halo[e, place, r : r + 1, :]

        zero = jnp.zeros((1, cells), jnp.float32)
        up_x = [jnp.where(at_last_x, zero, got(0, r)) for r in range(2)]
        up_y = [jnp.where(at_last_y, zero, got(2, r)) for r in range(2)]
        visc_x = jnp.where(at_first_x, zero, halo[0, 1, 2:3, :])
        visc_y = jnp.where(at_first_y, zero, halo[0, 3, 2:3, :])
        back_x = [got(1, r) for r in range(2)]
        back_y = [got(3, r) for r in range(2)]
        back_x_up, back_y_up = [], []
        for r in range(2):
            corner = jnp.where(at_last_y, 0.0, halo[e, 4, r : r + 1, 0:1])
            back_x_up.append(jnp.where(lane_of == cells - 1, corner, pltpu.roll(back_x[r], cells - 1, 1)))
            corner = jnp.where(at_last_x, 0.0, halo[e, 5, r : r + 1, cells - 1 : cells])
            back_y_up.append(jnp.where(lane_of == cells - 1, corner, pltpu.roll(back_y[r], cells - 1, 1)))
        sxx_x = visc_x * (4.0 * (u_first - back_x[0]) + 2.0 * (back_x_up[1] - back_x[1]))
        sxy_x = visc_x * ((back_x_up[0] - back_x[0]) + (v_first - back_x[1]))
        u_y, v_y = edge[e, 2, 0:1, :], edge[e, 2, 1:2, :]
        sxy_y = visc_y * ((u_y - back_y[0]) + (back_y_up[1] - back_y[1]))
        syy_y = visc_y * (4.0 * (v_y - back_y[1]) + 2.0 * (back_y_up[0] - back_y[0]))
        return up_x, up_y, visc_x, visc_y, sxx_x, sxy_x, sxy_y, syy_y

    def as_columns(*rows):
        zero = jnp.zeros((8 - len(rows), cells), jnp.float32)
        turned = jnp.concatenate([*rows, zero], axis=0).T
        return [turned[:, n : n + 1] for n in range(len(rows))]

    strip_row = lax.broadcasted_iota(jnp.int32, (STRIP, 1), 0)

    def upper_x(field, row):
        return jnp.where(strip_row == STRIP - 1, row, pltpu.roll(field, STRIP - 1, 0))

    def lower_x(field, row):
        return jnp.where(strip_row == 0, row, pltpu.roll(field, 1, 0))

    def upper_y(field, column):
        return jnp.where(lane_of == cells - 1, column, pltpu.roll(field, cells - 1, 1))

    def lower_y(field, column):
        return jnp.where(lane_of == 0, column, pltpu.roll(field, 1, 1))

    def stress_images(field, up_x, up_y, sxx_x, sxy_x, sxy_y, syy_y, apply):
        for i in range(0, cells, STRIP):
            rows_i = slice(i, i + STRIP)
            u, v = field(0, rows_i), field(1, rows_i)
            following = slice(i + STRIP, i + STRIP + 1)
            after = up_x if i + STRIP == cells else [field(r, following) for r in range(2)]
            a_x, b_x = upper_x(u, after[0]) - u, upper_x(v, after[1]) - v
            a_y = upper_y(u, take(up_y[0], rows_i)) - u
            b_y = upper_y(v, take(up_y[1], rows_i)) - v
            visc = visc_ref[rows_i, :]
            sxx = visc * (4.0 * a_x + 2.0 * b_y)
            syy = visc * (4.0 * b_y + 2.0 * a_x)
            sxy = visc * (a_y + b_x)
            push_u = lower_x(sxx, sxx_x) - sxx + lower_y(sxy, take(sxy_y, rows_i)) - sxy
            push_v = lower_x(sxy, sxy_x) - sxy + lower_y(syy, take(syy_y, rows_i)) - syy
            apply(rows_i, (u, v), (push_u, push_v))
            sxx_x, sxy_x = sxx[STRIP - 1 :, :], sxy[STRIP - 1 :, :]

    def take(column, rows_i):
        return column if isinstance(column, float) else column[rows_i, :]

    def ice_row(rows_i):
        s = rows_i.start // (cells // 2) * 2
        return jnp.where(lane_of < cells // 2, ice(s), ice(s + 1))

    def first_sweep():
        def field(r, rows_i):
            return vel_ref[r, rows_i, :].astype(jnp.float32)

        up_x, up_y, visc_x, visc_y, sxx_x, sxy_x, sxy_y, syy_y = outside(0, field(0, slice(0, 1)), field(1, slice(0, 1)))
        *columns, visc_y = as_columns(up_y[0], up_y[1], sxy_y, syy_y, visc_y)

        def apply(rows_i, start, push):
            visc, fric = visc_ref[rows_i, :], fric_ref[rows_i, :]
            before = visc_x if rows_i.start == 0 else visc_ref[rows_i.start - 1 : rows_i.start, :]
            behind_x, behind_y = lower_x(visc, before), lower_y(visc, visc_y[rows_i, :])
            diag = (5.0 * visc + 4.0 * behind_x + behind_y, 5.0 * visc + behind_x + 4.0 * behind_y)
            for r in range(2):
                relax_r = 1.0 / (diag[r] + fric)
                relax[r, rows_i, :] = OMEGA * relax_r
                moved = relax_r * (drive_ref[r, rows_i, :].astype(jnp.float32) - push[r] - fric * start[r])
                gain[r, rows_i, :] = ice_row(rows_i) * (OMEGA * relax_r) * (moved + start[r])
                first[r, rows_i, :] = start[r] + OMEGA * moved

        stress_images(field, up_x, columns[:2], sxx_x, sxy_x, columns[2], columns[3], apply)
        send_edges(1, first.at[0], first.at[1])

    def second_sweep():
        def field(r, rows_i):
            return first[r, rows_i, :]

        up_x, up_y, _, _, sxx_x, sxy_x, sxy_y, syy_y = outside(1, field(0, slice(0, 1)), field(1, slice(0, 1)))
        columns = as_columns(up_y[0], up_y[1], sxy_y, syy_y)

        def apply(rows_i, start, push):
            fric = fric_ref[rows_i, :]
            for r in range(2):
                residual = drive_ref[r, rows_i, :].astype(jnp.float32) - push[r] - fric * start[r]
                moved = relax[r, rows_i, :] * residual
                q_two[r, rows_i, :] = ice_row(rows_i) * ((1.0 / OMEGA) * moved + start[r])
                second[r, rows_i, :] = start[r] + moved

        stress_images(field, up_x, columns[:2], sxx_x, sxy_x, columns[2], columns[3], apply)
        gains = columns_of((False, gain.at[0]), (False, gain.at[1]), (True, gain.at[0]), (True, gain.at[1]))
        gain_edge[0:4, :] = gains[0:4]

    def adjoint():
        def field(r, rows_i):
            return lift[r, rows_i, :]

        send_columns(2, lift.at[0], lift.at[1])

        def apply(rows_i, lifted, push):
            fric = fric_ref[rows_i, :]
            total = None
            for r in range(2):
                back = push[r] - misfit[r, rows_i, :] + fric * lifted[r]
                term = gain[r, rows_i, :] * back - q_two[r, rows_i, :] * lifted[r]
                total = term if total is None else total + term
            out_ref[rows_i, :] = total

        zero = jnp.zeros((1, cells), jnp.float32)
        stress_images(field, (zero, zero), (0.0, 0.0), zero, zero, 0.0, 0.0, apply)
        wait_sends()
        up_x, up_y, _, _, sxx_x, sxy_x, sxy_y, syy_y = outside(2, field(0, slice(0, 1)), field(1, slice(0, 1)))
        end = slice(cells - 1, cells)
        visc = visc_ref[end, :]
        sxx, syy, sxy = 4.0 * visc * up_x[0], 2.0 * visc * up_x[0], visc * up_x[1]
        push_u = lower_y(sxy, 0.0) - sxy - sxx
        push_v = lower_y(syy, 0.0) - syy - sxy
        out_ref[0:1, :] += gain[0, 0:1, :] * sxx_x + gain[1, 0:1, :] * sxy_x
        out_ref[end, :] += gain[0, end, :] * push_u + gain[1, end, :] * push_v
        visc = edge[0, 3, 2:3, :]
        sxx, syy, sxy = 2.0 * visc * up_y[1], 4.0 * visc * up_y[1], visc * up_y[0]
        push_u = lower_y(sxx, 0.0) - sxx - sxy
        push_v = lower_y(sxy, 0.0) - sxy - syy
        column_first, column_last = as_columns(
            gain_edge[0:1, :] * sxy_y + gain_edge[1:2, :] * syy_y,
            gain_edge[2:3, :] * push_u + gain_edge[3:4, :] * push_v,
        )
        lane = lane_of[:, :128]
        out_ref[:, :128] += jnp.where(lane == 0, column_first, 0.0)
        out_ref[:, cells - 128 :] += jnp.where(lane == 127, column_last, 0.0)

    def ice(s):
        return ice_ref[s // 2, s % 2].astype(jnp.float32)

    width = scenes * ROWS
    diagonal = lax.broadcasted_iota(jnp.int32, (ROWS, width), 0) == lax.bitwise_and(
        lax.broadcasted_iota(jnp.int32, (ROWS, width), 1), ROWS - 1
    )

    def fill(source, block):
        key, weight = block[0:1, :], block[1:2, :]
        for distance in range(NZ):
            owner = lax.rem(z + distance, NZ) * NX + x
            for slot in range(SLOTS):
                want = (owner * SLOTS + slot).astype(jnp.float32)
                chosen = jnp.where(key == want, weight, 0.0)
                at = (distance * SLOTS + slot) * ROWS
                table[at : at + ROWS, source * width : (source + 1) * width] = jnp.where(
                    diagonal, chosen, 0.0
                ).astype(jnp.bfloat16)

    for load in loads[3:]:
        load.wait()
    send_edges(0, vel_ref[0].astype(jnp.float32), vel_ref[1].astype(jnp.float32), visc_ref)
    fill(0, meta_ref[...])
    for peer in range(3):
        meta_send(peer).wait_recv()
        fill(1 + peer, meta[peer])
    ones = jnp.ones((4 * width, 128), jnp.bfloat16)
    total_w = jnp.dot(table[...], ones, preferred_element_type=jnp.float32)
    part_w[...] = jnp.zeros_like(part_w)
    for distance in range(NZ):
        for slot in range(SLOTS):
            at = (distance * SLOTS + slot) * ROWS
            place = NZ if distance == NZ // 2 and slot >= 2 else distance
            part_w[place, slot : slot + 1, :] = total_w[at : at + 1, :]
    ring_send_w(0, 1).start()
    ring_send_w(1, 1).start()
    for c in range(chunks):
        own_load(c).wait()
    def at_chunk(c, action):
        pl.when(jnp.logical_and(c >= 0, c < chunks))(lambda: action(c))

    def combine(c):
        for side in range(2):
            far_send(side, c).wait_recv()
        columns = []
        for h in range(ROWS // 16):
            columns.append(
                jnp.concatenate(
                    [ag[s, c, :, h * 16 : (h + 1) * 16, :].reshape(scenes * 16, 128) for s in range(4)], axis=0
                )
            )
        stacked = columns[0] if len(columns) == 1 else jnp.concatenate(columns, axis=1)
        sums = jnp.dot(table[...], stacked, preferred_element_type=jnp.float32)
        part[c] = sums.reshape(NZ, SLOTS, ROWS, 128)
        ring_send(0, 1, c).start()
        ring_send(1, 1, c).start()

    def ring_step(stage, c):
        for side in range(2):
            ring_send(side, stage - 1, c).wait_recv()
            mine = 5 - stage if side == 0 else 3 + stage
            if stage == 2:
                part[c, mine, side * 2 : side * 2 + 2] += (rp1, rm1)[side][c]
            else:
                part[c, mine] += (rp, rm)[side][stage - 3, c]
            ring_send(side, stage, c).start()

    def finish(c):
        for side in range(2):
            ring_send(side, 4, c).wait_recv()
        obs_sum = part[c, 0] + (rp[2, c] + rm[2, c])
        tile = cells // 2
        component, offset = component_of(c), offset_of(c)
        for s in range(SLOTS):
            at = (
                component,
                pl.ds(pl.multiple_of(s // 2 * tile + offset, ROWS), ROWS),
                slice(s % 2 * tile, s % 2 * tile + tile),
            )
            value = ice(s) * (part_w[0, s : s + 1, :] * second[at] - obs_sum[s])
            misfit[at] = value
            lift[at] = relax[at] * value

    def ring_step_w(stage):
        for side in range(2):
            ring_send_w(side, stage - 1).wait_recv()
            mine = 5 - stage if side == 0 else 3 + stage
            part_w[mine] += rw[side * 4 + stage - 2]
            ring_send_w(side, stage).start()

    def finish_w():
        for side in range(2):
            ring_send_w(side, 4).wait_recv()
        part_w[0] += rw[3] + rw[7]

    def drain(c):
        for side in range(2):
            own_send(side, c).wait_send()
            far_send(side, c).wait_send()
            for stage in range(1, 5):
                ring_send(side, stage, c).wait_send()

    def wait_sends():
        drain(chunks - 1)
        for peer in range(3):
            meta_send(peer).wait_send()
        for side in range(2):
            for stage in range(1, 5):
                ring_send_w(side, stage).wait_send()

    def step(k, carry):
        @pl.when(k < chunks)
        def _():
            for side in range(2):
                own_send(side, k).wait_recv()
                far_send(side, k).start()

        @pl.when(k + LEAD < chunks)
        def _():
            own_send(0, k + LEAD).start()
            own_send(1, k + LEAD).start()

        pl.when(k == 1 + 4 * GAP)(finish_w)
        at_chunk(k - 1 - 4 * GAP, finish)
        at_chunk(k - 2 - 4 * GAP, drain)
        pl.when(k == 4 + 4 * GAP)(lambda: send_rows(2, lift.at[0], lift.at[1]))
        for stage in (4, 3, 2):
            at_chunk(k - 1 - (stage - 1) * GAP, functools.partial(ring_step, stage))
            pl.when(k == 2 * stage - 3)(functools.partial(ring_step_w, stage))
        at_chunk(k - 1, combine)
        pl.when(k == 0)(first_sweep)
        pl.when(k == 2)(second_sweep)
        return carry

    lax.fori_loop(0, chunks + 1 + 4 * GAP, step, 0)
    adjoint()
    for e in range(3):
        for place in range(6):
            edge_send(e, place).wait_send()


def body(vel0, visc, fric, drive, scene_obs, scene_weight, scene_owner, scene_slot, ice_mask):
    obs = scene_obs[0]
    cells = visc.shape[0]
    scenes, _, tile, _ = obs.shape
    height = 2 * tile
    chunks = height // ROWS
    f32, bf16 = jnp.float32, jnp.bfloat16
    dma = pltpu.SemaphoreType.DMA
    return pl.pallas_call(
        exchange_kernel,
        out_shape=jax.ShapeDtypeStruct((cells, cells), f32),
        in_specs=[
            pl.BlockSpec(memory_space=pltpu.HBM)
        ] * 9,
        out_specs=pl.BlockSpec(memory_space=pltpu.VMEM),
        scratch_shapes=[
            pltpu.VMEM((1, scenes), jnp.int32),
            pltpu.VMEM((1, scenes), jnp.int32),
            pltpu.VMEM((1, scenes), bf16),
            pltpu.SMEM((2, 2), jnp.int32),
            pltpu.VMEM((2, cells, cells), bf16),
            pltpu.VMEM((cells, cells), f32),
            pltpu.VMEM((cells, cells), f32),
            pltpu.VMEM((2, cells, cells), bf16),
            pltpu.VMEM((8, scenes * ROWS), f32),
            *[pltpu.VMEM((2, cells, cells), f32)] * 7,
            pltpu.VMEM((3, 4, 8, cells), f32),
            pltpu.VMEM((3, 6, 8, cells), f32),
            pltpu.VMEM((8, cells), f32),
            pltpu.VMEM((3, 8, scenes * ROWS), f32),
            pltpu.VMEM((4, chunks, scenes, ROWS, tile), bf16),
            pltpu.VMEM((NZ * SLOTS * ROWS, 4 * scenes * ROWS), bf16),
            pltpu.VMEM((chunks, NZ, SLOTS, ROWS, tile), f32),
            pltpu.VMEM((NZ + 1, 8, 128), f32),
            pltpu.VMEM((chunks, 2, ROWS, tile), f32),
            pltpu.VMEM((3, chunks, SLOTS, ROWS, tile), f32),
            pltpu.VMEM((chunks, 2, ROWS, tile), f32),
            pltpu.VMEM((3, chunks, SLOTS, ROWS, tile), f32),
            pltpu.VMEM((8, 8, 128), f32),
            dma((chunks,)),
            dma((3,)), dma((3,)),
            dma((4, chunks)), dma((4, chunks)),
            dma((8, chunks)), dma((8, chunks)),
            dma((8,)), dma((8,)),
            dma((3, 6)), dma((3, 6)),
            dma((8,)),
        ],
        compiler_params=pltpu.CompilerParams(
            collective_id=0, has_side_effects=True, vmem_limit_bytes=67043328
        ),
    )(scene_owner.reshape(1, scenes), scene_slot, scene_weight, ice_mask, vel0, visc, fric, drive, obs.reshape(scenes, height, tile))


def solution(mesh):
    placed = (
        P(None, "gx", "gy"),
        P("gx", "gy"),
        P("gx", "gy"),
        P(None, "gx", "gy"),
        P("gy", "gx", None, None, None),
        P("gy", "gx"),
        P("gy", "gx", None),
        P("gy", "gx"),
        P("gx", "gy"),
    )
    return jax.shard_map(body, mesh=mesh, in_specs=placed, out_specs=P("gx", "gy"), check_vma=False)
```

```python
import functools

import jax
import jax.numpy as jnp
from jax import lax
from jax.experimental import pallas as pl
from jax.experimental.pallas import tpu as pltpu
from jax.sharding import PartitionSpec as P

OMEGA = 0.6
NX, NZ = 4, 8
SLOTS = 4
STRIP = 32
ROWS = 16
LEAD = 3
GAP = 2
MESH = pl.DeviceIdType.MESH


def exchange_kernel(
    owner_in, slot_in, weight_in, ice_in, vel_in, visc_in, fric_in, drive_in, obs_ref, out_ref,
    owner_ref, slot_ref, weight_ref, ice_ref, vel_ref, visc_ref, fric_ref, drive_ref, meta_ref,
    relax, first, second, gain, q_two, misfit, lift, edge, halo, gain_edge,
    meta, ag, table, part, part_w, rp1, rp, rm1, rm, rw,
    own_sem, meta_s, meta_r, ag_s, ag_r, rs_s, rs_r, rw_s, rw_r, edge_s, edge_r, load_sem,
):
    chunks = ag.shape[1]
    scenes = ag.shape[2]
    half = scenes // 2
    me_x, me_y = lax.axis_index("gx"), lax.axis_index("gy")
    x, z = lax.rem(me_x, NX), me_x // NX
    x_right = (z * NX + lax.rem(x + 1, NX), me_y)
    x_left = (z * NX + lax.rem(x + NX - 1, NX), me_y)
    x_far = (z * NX + lax.rem(x + 2, NX), me_y)
    z_right = (lax.rem(z + 1, NZ) * NX + x, me_y)
    z_left = (lax.rem(z + NZ - 1, NZ) * NX + x, me_y)

    gx_next, gx_back = lax.rem(me_x + 1, NX * NZ), lax.rem(me_x + NX * NZ - 1, NX * NZ)
    side_y = lax.axis_size("gy")
    gy_next, gy_back = lax.rem(me_y + 1, side_y), lax.rem(me_y + side_y - 1, side_y)
    at_first_x, at_last_x = me_x == 0, me_x == NX * NZ - 1
    at_first_y, at_last_y = me_y == 0, me_y == side_y - 1
    edges = (
        (0, (gx_back, me_y)),
        (1, (gx_next, me_y)),
        (2, (me_x, gy_back)),
        (3, (me_x, gy_next)),
        (1, (gx_next, gy_back)),
        (0, (gx_back, gy_next)),
    )

    def remote(src, dst, send, recv, device):
        return pltpu.make_async_remote_copy(
            src_ref=src, dst_ref=dst, send_sem=send, recv_sem=recv, device_id=device, device_id_type=MESH
        )

    def component_of(c):
        return lax.rem(c, 2)

    def offset_of(c):
        return lax.rem((c // 2) * (chunks // 2 - 1), chunks // 2) * ROWS

    def rows(c):
        start = component_of(c) * (chunks // 2 * ROWS) + offset_of(c)
        return pl.ds(pl.multiple_of(start, ROWS), ROWS)

    def own_load(c):
        return pltpu.make_async_copy(obs_ref.at[:, rows(c), :], ag.at[0, c], own_sem.at[c])

    def own_send(side, c):
        return remote(
            obs_ref.at[:, rows(c), :], ag.at[1 + side, c], ag_s.at[side, c], ag_r.at[side, c],
            (x_right, x_left)[side],
        )

    def far_send(side, c):
        piece = pl.ds(side * half, half)
        return remote(
            ag.at[1 + side, c, piece], ag.at[3, c, piece], ag_s.at[2 + side, c], ag_r.at[2 + side, c],
            (x_right, x_left)[side],
        )

    def meta_send(peer):
        return remote(
            meta_ref, meta.at[peer], meta_s.at[peer], meta_r.at[peer], (x_right, x_left, x_far)[peer]
        )

    def ring_send(side, stage, c):
        device = (z_right, z_left)[side]
        semaphores = (rs_s.at[side * 4 + stage - 1, c], rs_r.at[side * 4 + stage - 1, c])
        if stage == 1:
            return remote(
                part.at[c, 4, pl.ds(side * 2, 2)], (rp1, rm1)[side].at[c], *semaphores, device
            )
        source = 5 - stage if side == 0 else 3 + stage
        return remote(part.at[c, source], (rp, rm)[side].at[stage - 2, c], *semaphores, device)

    def ring_send_w(side, stage):
        source = 5 - stage if side == 0 else (8 if stage == 1 else 3 + stage)
        index = side * 4 + stage - 1
        return remote(
            part_w.at[source], rw.at[index], rw_s.at[index], rw_r.at[index], (z_right, z_left)[side]
        )

    def edge_send(e, place):
        message, device = edges[place]
        return remote(
            edge.at[e, message], halo.at[e, place], edge_s.at[e, place], edge_r.at[e, place], device
        )

    barrier = pltpu.get_barrier_semaphore()
    for device in (x_right, x_left, x_far, z_right, z_left, *(device for _, device in edges)):
        pl.semaphore_signal(barrier, inc=1, device_id=device, device_id_type=MESH)
    pairs = (
        (owner_in, owner_ref), (slot_in, slot_ref), (weight_in, weight_ref), (vel_in, vel_ref),
        (visc_in, visc_ref), (fric_in, fric_ref), (drive_in, drive_ref), (ice_in, ice_ref),
    )
    loads = [pltpu.make_async_copy(a, b, load_sem.at[n]) for n, (a, b) in enumerate(pairs)]
    for load in loads:
        load.start()
    for c in range(chunks):
        own_load(c).start()
    for load in loads[:3]:
        load.wait()
    key = (owner_ref[...] * SLOTS + slot_ref[...]).astype(jnp.float32)
    place = lax.broadcasted_iota(jnp.int32, (scenes, scenes), 0)
    same = place == lax.broadcasted_iota(jnp.int32, (scenes, scenes), 1)
    spread = lax.broadcasted_iota(jnp.int32, (scenes, scenes * ROWS), 1) // ROWS
    spread = spread == lax.broadcasted_iota(jnp.int32, (scenes, scenes * ROWS), 0)
    for r, value in enumerate((key, weight_ref[...].astype(jnp.float32))):
        column = jnp.sum(jnp.where(same, value, 0.0), axis=1, keepdims=True)
        meta_ref[r : r + 1, :] = jnp.sum(jnp.where(spread, column, 0.0), axis=0, keepdims=True)
    pl.semaphore_wait(barrier, 11)

    for peer in range(3):
        meta_send(peer).start()
    for c in range(LEAD):
        own_send(0, c).start()
        own_send(1, c).start()

    cells = visc_ref.shape[0]
    lane_of = lax.broadcasted_iota(jnp.int32, (1, cells), 1)

    def columns_of(*columns):
        lane, packed = lane_of[:, :128], None
        for n, (last, array) in enumerate(columns):
            block = array[:, cells - 128 :] if last else array[:, :128]
            moved = (n + 1 if last else n) % 128
            block = pltpu.roll(block, moved, 1) if moved else block
            packed = block if packed is None else jnp.where(lane == n, block, packed)
        return packed.T

    def send_rows(e, u, v, visc=None):
        for r, array in enumerate((u, v)):
            edge[e, 0, r : r + 1, :] = array[0:1, :]
            edge[e, 1, r : r + 1, :] = array[cells - 1 :, :]
        if visc is not None:
            edge[e, 1, 2:3, :] = visc[cells - 1 :, :]
        for place in (0, 1, 4, 5):
            edge_send(e, place).start()

    def send_columns(e, u, v, visc=None):
        columns = [(False, u), (False, v), (True, u), (True, v)]
        if visc is not None:
            columns.append((True, visc))
        turned = columns_of(*columns)
        edge[e, 2, 0:2, :] = turned[0:2]
        edge[e, 3, 0:3, :] = turned[2:5]
        for place in (2, 3):
            edge_send(e, place).start()

    def send_edges(*field):
        send_rows(*field)
        send_columns(*field)

    def outside(e, u_first, v_first):
        for place in range(6):
            edge_send(e, place).wait_recv()

        def got(place, r):
            return halo[e, place, r : r + 1, :]

        zero = jnp.zeros((1, cells), jnp.float32)
        up_x = [jnp.where(at_last_x, zero, got(0, r)) for r in range(2)]
        up_y = [jnp.where(at_last_y, zero, got(2, r)) for r in range(2)]
        visc_x = jnp.where(at_first_x, zero, halo[0, 1, 2:3, :])
        visc_y = jnp.where(at_first_y, zero, halo[0, 3, 2:3, :])
        back_x = [got(1, r) for r in range(2)]
        back_y = [got(3, r) for r in range(2)]
        back_x_up, back_y_up = [], []
        for r in range(2):
            corner = jnp.where(at_last_y, 0.0, halo[e, 4, r : r + 1, 0:1])
            back_x_up.append(jnp.where(lane_of == cells - 1, corner, pltpu.roll(back_x[r], cells - 1, 1)))
            corner = jnp.where(at_last_x, 0.0, halo[e, 5, r : r + 1, cells - 1 : cells])
            back_y_up.append(jnp.where(lane_of == cells - 1, corner, pltpu.roll(back_y[r], cells - 1, 1)))
        sxx_x = visc_x * (4.0 * (u_first - back_x[0]) + 2.0 * (back_x_up[1] - back_x[1]))
        sxy_x = visc_x * ((back_x_up[0] - back_x[0]) + (v_first - back_x[1]))
        u_y, v_y = edge[e, 2, 0:1, :], edge[e, 2, 1:2, :]
        sxy_y = visc_y * ((u_y - back_y[0]) + (back_y_up[1] - back_y[1]))
        syy_y = visc_y * (4.0 * (v_y - back_y[1]) + 2.0 * (back_y_up[0] - back_y[0]))
        return up_x, up_y, visc_x, visc_y, sxx_x, sxy_x, sxy_y, syy_y

    def as_columns(*rows):
        zero = jnp.zeros((8 - len(rows), cells), jnp.float32)
        turned = jnp.concatenate([*rows, zero], axis=0).T
        return [turned[:, n : n + 1] for n in range(len(rows))]

    strip_row = lax.broadcasted_iota(jnp.int32, (STRIP, 1), 0)

    def upper_x(field, row):
        return jnp.where(strip_row == STRIP - 1, row, pltpu.roll(field, STRIP - 1, 0))

    def lower_x(field, row):
        return jnp.where(strip_row == 0, row, pltpu.roll(field, 1, 0))

    def upper_y(field, column):
        return jnp.where(lane_of == cells - 1, column, pltpu.roll(field, cells - 1, 1))

    def lower_y(field, column):
        return jnp.where(lane_of == 0, column, pltpu.roll(field, 1, 1))

    def stress_images(field, up_x, up_y, sxx_x, sxy_x, sxy_y, syy_y, apply):
        for i in range(0, cells, STRIP):
            rows_i = slice(i, i + STRIP)
            u, v = field(0, rows_i), field(1, rows_i)
            following = slice(i + STRIP, i + STRIP + 1)
            after = up_x if i + STRIP == cells else [field(r, following) for r in range(2)]
            a_x, b_x = upper_x(u, after[0]) - u, upper_x(v, after[1]) - v
            a_y = upper_y(u, take(up_y[0], rows_i)) - u
            b_y = upper_y(v, take(up_y[1], rows_i)) - v
            visc = visc_ref[rows_i, :]
            sxx = visc * (4.0 * a_x + 2.0 * b_y)
            syy = visc * (4.0 * b_y + 2.0 * a_x)
            sxy = visc * (a_y + b_x)
            push_u = lower_x(sxx, sxx_x) - sxx + lower_y(sxy, take(sxy_y, rows_i)) - sxy
            push_v = lower_x(sxy, sxy_x) - sxy + lower_y(syy, take(syy_y, rows_i)) - syy
            apply(rows_i, (u, v), (push_u, push_v))
            sxx_x, sxy_x = sxx[STRIP - 1 :, :], sxy[STRIP - 1 :, :]

    def take(column, rows_i):
        return column if isinstance(column, float) else column[rows_i, :]

    def ice_row(rows_i):
        s = rows_i.start // (cells // 2) * 2
        return jnp.where(lane_of < cells // 2, ice(s), ice(s + 1))

    def first_sweep():
        def field(r, rows_i):
            return vel_ref[r, rows_i, :].astype(jnp.float32)

        up_x, up_y, visc_x, visc_y, sxx_x, sxy_x, sxy_y, syy_y = outside(0, field(0, slice(0, 1)), field(1, slice(0, 1)))
        *columns, visc_y = as_columns(up_y[0], up_y[1], sxy_y, syy_y, visc_y)

        def apply(rows_i, start, push):
            visc, fric = visc_ref[rows_i, :], fric_ref[rows_i, :]
            before = visc_x if rows_i.start == 0 else visc_ref[rows_i.start - 1 : rows_i.start, :]
            behind_x, behind_y = lower_x(visc, before), lower_y(visc, visc_y[rows_i, :])
            diag = (5.0 * visc + 4.0 * behind_x + behind_y, 5.0 * visc + behind_x + 4.0 * behind_y)
            for r in range(2):
                relax_r = 1.0 / (diag[r] + fric)
                relax[r, rows_i, :] = OMEGA * relax_r
                moved = relax_r * (drive_ref[r, rows_i, :].astype(jnp.float32) - push[r] - fric * start[r])
                gain[r, rows_i, :] = ice_row(rows_i) * (OMEGA * relax_r) * (moved + start[r])
                first[r, rows_i, :] = start[r] + OMEGA * moved

        stress_images(field, up_x, columns[:2], sxx_x, sxy_x, columns[2], columns[3], apply)
        send_edges(1, first.at[0], first.at[1])

    def second_sweep():
        def field(r, rows_i):
            return first[r, rows_i, :]

        up_x, up_y, _, _, sxx_x, sxy_x, sxy_y, syy_y = outside(1, field(0, slice(0, 1)), field(1, slice(0, 1)))
        columns = as_columns(up_y[0], up_y[1], sxy_y, syy_y)

        def apply(rows_i, start, push):
            fric = fric_ref[rows_i, :]
            for r in range(2):
                residual = drive_ref[r, rows_i, :].astype(jnp.float32) - push[r] - fric * start[r]
                moved = relax[r, rows_i, :] * residual
                q_two[r, rows_i, :] = ice_row(rows_i) * ((1.0 / OMEGA) * moved + start[r])
                second[r, rows_i, :] = start[r] + moved

        stress_images(field, up_x, columns[:2], sxx_x, sxy_x, columns[2], columns[3], apply)
        gains = columns_of((False, gain.at[0]), (False, gain.at[1]), (True, gain.at[0]), (True, gain.at[1]))
        gain_edge[0:4, :] = gains[0:4]

    def adjoint():
        def field(r, rows_i):
            return lift[r, rows_i, :]

        send_columns(2, lift.at[0], lift.at[1])

        def apply(rows_i, lifted, push):
            fric = fric_ref[rows_i, :]
            total = None
            for r in range(2):
                back = push[r] - misfit[r, rows_i, :] + fric * lifted[r]
                term = gain[r, rows_i, :] * back - q_two[r, rows_i, :] * lifted[r]
                total = term if total is None else total + term
            out_ref[rows_i, :] = total

        zero = jnp.zeros((1, cells), jnp.float32)
        stress_images(field, (zero, zero), (0.0, 0.0), zero, zero, 0.0, 0.0, apply)
        wait_sends()
        up_x, up_y, _, _, sxx_x, sxy_x, sxy_y, syy_y = outside(2, field(0, slice(0, 1)), field(1, slice(0, 1)))
        end = slice(cells - 1, cells)
        visc = visc_ref[end, :]
        sxx, syy, sxy = 4.0 * visc * up_x[0], 2.0 * visc * up_x[0], visc * up_x[1]
        push_u = lower_y(sxy, 0.0) - sxy - sxx
        push_v = lower_y(syy, 0.0) - syy - sxy
        out_ref[0:1, :] += gain[0, 0:1, :] * sxx_x + gain[1, 0:1, :] * sxy_x
        out_ref[end, :] += gain[0, end, :] * push_u + gain[1, end, :] * push_v
        visc = edge[0, 3, 2:3, :]
        sxx, syy, sxy = 2.0 * visc * up_y[1], 4.0 * visc * up_y[1], visc * up_y[0]
        push_u = lower_y(sxx, 0.0) - sxx - sxy
        push_v = lower_y(sxy, 0.0) - sxy - syy
        column_first, column_last = as_columns(
            gain_edge[0:1, :] * sxy_y + gain_edge[1:2, :] * syy_y,
            gain_edge[2:3, :] * push_u + gain_edge[3:4, :] * push_v,
        )
        lane = lane_of[:, :128]
        out_ref[:, :128] += jnp.where(lane == 0, column_first, 0.0)
        out_ref[:, cells - 128 :] += jnp.where(lane == 127, column_last, 0.0)

    def ice(s):
        return ice_ref[s // 2, s % 2].astype(jnp.float32)

    width = scenes * ROWS
    diagonal = lax.broadcasted_iota(jnp.int32, (ROWS, width), 0) == lax.bitwise_and(
        lax.broadcasted_iota(jnp.int32, (ROWS, width), 1), ROWS - 1
    )

    def fill(source, block):
        key, weight = block[0:1, :], block[1:2, :]
        for distance in range(NZ):
            owner = lax.rem(z + distance, NZ) * NX + x
            for slot in range(SLOTS):
                want = (owner * SLOTS + slot).astype(jnp.float32)
                chosen = jnp.where(key == want, weight, 0.0)
                at = (distance * SLOTS + slot) * ROWS
                table[at : at + ROWS, source * width : (source + 1) * width] = jnp.where(
                    diagonal, chosen, 0.0
                ).astype(jnp.bfloat16)

    for load in loads[3:]:
        load.wait()
    send_edges(0, vel_ref[0].astype(jnp.float32), vel_ref[1].astype(jnp.float32), visc_ref)
    fill(0, meta_ref[...])
    for peer in range(3):
        meta_send(peer).wait_recv()
        fill(1 + peer, meta[peer])
    ones = jnp.ones((4 * width, 128), jnp.bfloat16)
    total_w = jnp.dot(table[...], ones, preferred_element_type=jnp.float32)
    part_w[...] = jnp.zeros_like(part_w)
    for distance in range(NZ):
        for slot in range(SLOTS):
            at = (distance * SLOTS + slot) * ROWS
            place = NZ if distance == NZ // 2 and slot >= 2 else distance
            part_w[place, slot : slot + 1, :] = total_w[at : at + 1, :]
    ring_send_w(0, 1).start()
    ring_send_w(1, 1).start()
    for c in range(chunks):
        own_load(c).wait()
    def at_chunk(c, action):
        pl.when(jnp.logical_and(c >= 0, c < chunks))(lambda: action(c))

    def combine(c):
        for side in range(2):
            far_send(side, c).wait_recv()
        columns = []
        for h in range(ROWS // 16):
            columns.append(
                jnp.concatenate(
                    [ag[s, c, :, h * 16 : (h + 1) * 16, :].reshape(scenes * 16, 128) for s in range(4)], axis=0
                )
            )
        stacked = columns[0] if len(columns) == 1 else jnp.concatenate(columns, axis=1)
        sums = jnp.dot(table[...], stacked, preferred_element_type=jnp.float32)
        part[c] = sums.reshape(NZ, SLOTS, ROWS, 128)
        ring_send(0, 1, c).start()
        ring_send(1, 1, c).start()

    def ring_step(stage, c):
        for side in range(2):
            ring_send(side, stage - 1, c).wait_recv()
            mine = 5 - stage if side == 0 else 3 + stage
            if stage == 2:
                part[c, mine, side * 2 : side * 2 + 2] += (rp1, rm1)[side][c]
            else:
                part[c, mine] += (rp, rm)[side][stage - 3, c]
            ring_send(side, stage, c).start()

    def finish(c):
        for side in range(2):
            ring_send(side, 4, c).wait_recv()
        obs_sum = part[c, 0] + (rp[2, c] + rm[2, c])
        tile = cells // 2
        component, offset = component_of(c), offset_of(c)
        for s in range(SLOTS):
            at = (
                component,
                pl.ds(pl.multiple_of(s // 2 * tile + offset, ROWS), ROWS),
                slice(s % 2 * tile, s % 2 * tile + tile),
            )
            value = ice(s) * (part_w[0, s : s + 1, :] * second[at] - obs_sum[s])
            misfit[at] = value
            lift[at] = relax[at] * value

    def ring_step_w(stage):
        for side in range(2):
            ring_send_w(side, stage - 1).wait_recv()
            mine = 5 - stage if side == 0 else 3 + stage
            part_w[mine] += rw[side * 4 + stage - 2]
            ring_send_w(side, stage).start()

    def finish_w():
        for side in range(2):
            ring_send_w(side, 4).wait_recv()
        part_w[0] += rw[3] + rw[7]

    def drain(c):
        for side in range(2):
            own_send(side, c).wait_send()
            far_send(side, c).wait_send()
            for stage in range(1, 5):
                ring_send(side, stage, c).wait_send()

    def wait_sends():
        drain(chunks - 1)
        for peer in range(3):
            meta_send(peer).wait_send()
        for side in range(2):
            for stage in range(1, 5):
                ring_send_w(side, stage).wait_send()

    def step(k, carry):
        @pl.when(k < chunks)
        def _():
            for side in range(2):
                own_send(side, k).wait_recv()
                far_send(side, k).start()

        @pl.when(k + LEAD < chunks)
        def _():
            own_send(0, k + LEAD).start()
            own_send(1, k + LEAD).start()

        pl.when(k == 1 + 4 * GAP)(finish_w)
        at_chunk(k - 1 - 4 * GAP, finish)
        at_chunk(k - 2 - 4 * GAP, drain)
        pl.when(k == 4 + 4 * GAP)(lambda: send_rows(2, lift.at[0], lift.at[1]))
        for stage in (4, 3, 2):
            at_chunk(k - 1 - (stage - 1) * GAP, functools.partial(ring_step, stage))
            pl.when(k == 2 * stage - 3)(functools.partial(ring_step_w, stage))
        at_chunk(k - 1, combine)
        pl.when(k == 2)(first_sweep)
        pl.when(k == 6)(second_sweep)
        return carry

    lax.fori_loop(0, chunks + 1 + 4 * GAP, step, 0)
    adjoint()
    for e in range(3):
        for place in range(6):
            edge_send(e, place).wait_send()


def body(vel0, visc, fric, drive, scene_obs, scene_weight, scene_owner, scene_slot, ice_mask):
    obs = scene_obs[0]
    cells = visc.shape[0]
    scenes, _, tile, _ = obs.shape
    height = 2 * tile
    chunks = height // ROWS
    f32, bf16 = jnp.float32, jnp.bfloat16
    dma = pltpu.SemaphoreType.DMA
    return pl.pallas_call(
        exchange_kernel,
        out_shape=jax.ShapeDtypeStruct((cells, cells), f32),
        in_specs=[
            pl.BlockSpec(memory_space=pltpu.HBM)
        ] * 9,
        out_specs=pl.BlockSpec(memory_space=pltpu.VMEM),
        scratch_shapes=[
            pltpu.VMEM((1, scenes), jnp.int32),
            pltpu.VMEM((1, scenes), jnp.int32),
            pltpu.VMEM((1, scenes), bf16),
            pltpu.SMEM((2, 2), jnp.int32),
            pltpu.VMEM((2, cells, cells), bf16),
            pltpu.VMEM((cells, cells), f32),
            pltpu.VMEM((cells, cells), f32),
            pltpu.VMEM((2, cells, cells), bf16),
            pltpu.VMEM((8, scenes * ROWS), f32),
            *[pltpu.VMEM((2, cells, cells), f32)] * 7,
            pltpu.VMEM((3, 4, 8, cells), f32),
            pltpu.VMEM((3, 6, 8, cells), f32),
            pltpu.VMEM((8, cells), f32),
            pltpu.VMEM((3, 8, scenes * ROWS), f32),
            pltpu.VMEM((4, chunks, scenes, ROWS, tile), bf16),
            pltpu.VMEM((NZ * SLOTS * ROWS, 4 * scenes * ROWS), bf16),
            pltpu.VMEM((chunks, NZ, SLOTS, ROWS, tile), f32),
            pltpu.VMEM((NZ + 1, 8, 128), f32),
            pltpu.VMEM((chunks, 2, ROWS, tile), f32),
            pltpu.VMEM((3, chunks, SLOTS, ROWS, tile), f32),
            pltpu.VMEM((chunks, 2, ROWS, tile), f32),
            pltpu.VMEM((3, chunks, SLOTS, ROWS, tile), f32),
            pltpu.VMEM((8, 8, 128), f32),
            dma((chunks,)),
            dma((3,)), dma((3,)),
            dma((4, chunks)), dma((4, chunks)),
            dma((8, chunks)), dma((8, chunks)),
            dma((8,)), dma((8,)),
            dma((3, 6)), dma((3, 6)),
            dma((8,)),
        ],
        compiler_params=pltpu.CompilerParams(
            collective_id=0, has_side_effects=True, vmem_limit_bytes=67043328
        ),
    )(scene_owner.reshape(1, scenes), scene_slot, scene_weight, ice_mask, vel0, visc, fric, drive, obs.reshape(scenes, height, tile))


def solution(mesh):
    placed = (
        P(None, "gx", "gy"),
        P("gx", "gy"),
        P("gx", "gy"),
        P(None, "gx", "gy"),
        P("gy", "gx", None, None, None),
        P("gy", "gx"),
        P("gy", "gx", None),
        P("gy", "gx"),
        P("gx", "gy"),
    )
    return jax.shard_map(body, mesh=mesh, in_specs=placed, out_specs=P("gx", "gy"), check_vma=False)
```
